768 devices in a mesh: seq: 4 (over z_hi), expert: 48 (over y, z_lo, core), rep: 4 (over x).
Axes of the slice: x: 4, y: 8, z: 12 (z_hi: 4, z_lo: 3; z = z_hi * 3 + z_lo), core: 2. Of those that a mesh axis runs over, the one named last changes fastest.
Arguments:
- query_rows: bfloat16 [48, 2048, 512], P('expert', ('seq', 'rep')), may hold values from -150 to 150
- key_rows: bfloat16 [48, 2048, 512], P('expert', ('seq', 'rep')), may hold values from -150 to 150
- value_rows: bfloat16 [48, 2048, 512], P('expert', ('seq', 'rep')), may hold values from -6 to 6
- doc_lengths: int32 [48, 8], P('expert'), may hold values from 1 to 1024, 2048 in all within a row
- residual: bfloat16 [48, 2048, 512], P('expert', ('seq', 'rep')), may hold values from -6 to 6
- out_proj: bfloat16 [512, 512], replicated, may hold values from -0.25 to 0.25
- router: bfloat16 [512, 48], replicated, may hold values from -0.5 to 0.5
- expert_choice: int32 [48, 2048, 1], P('expert', ('seq', 'rep')), may hold values from 0 to 47, as said below
- weight_in: bfloat16 [48, 512, 512], P('expert'), may hold values from -0.25 to 0.25
- weight_out: bfloat16 [48, 512, 512], P('expert'), may hold values from -0.5 to 0.5
- grad_out: bfloat16 [48, 2048, 512], P('expert', ('seq', 'rep')), may hold values from -6 to 6
Outputs:
- layer_out: bfloat16 [48, 2048, 512], P('expert', ('seq', 'rep'))
- grad_mixed: bfloat16 [48, 2048, 512], P('expert', ('seq', 'rep'))
- grad_weight_in: float32 [48, 512, 512], P('expert', ('seq', 'rep'))
- grad_weight_out: float32 [48, 512, 512], P('expert', ('seq', 'rep'))
The draws below stay inside these ranges and needn't reach their ends.
Inputs may be any that keep to these rules, and one draw needn't show every extreme that they name: `expert_choice`: A routing group is one index of seq and one of rep; each group has one hot expert, the same on all of the group's devices. Among one device's tokens, its group's hot expert is named between 5 and 16 times, exactly 16 times on some device and 4 + 1 times on some device; every other expert is named at most 4 times, and on every device some expert other than the hot one is named exactly 4 times. `doc_lengths`: each sequence's lengths sum to 2048; the longest is exactly half of 2048.
All inputs are finite; a program needn't handle non-finite values.
Results may differ from the reference program's by a relative error of at most 0.02.
Values may be sent and summed in bfloat16 or wider, within the bound.
A program may use at most 32 MiB of HBM per device.

```python
import math
import jax
import jax.numpy as jnp
import numpy as np
from jax import lax

D = 512
H = 16
HD = 32
FF = 512
DOCS = 8
TOK_DEV = 128
SEQ_LEN = 2048
SEQS = 48
EXPERTS = 48
CAP = 4
HOT_CAP = 16
N_SEQ = 4
N_REP = 4


def paired_rows(key):
    query_key, key_key = jax.random.split(jax.random.fold_in(key, 17))
    queries = jnp.clip(jax.random.normal(query_key, (SEQS, SEQ_LEN, D), jnp.float32), -4.0, 4.0)
    keyed = jnp.clip(jax.random.normal(key_key, (SEQS, SEQ_LEN, D), jnp.float32), -4.0, 4.0)
    return (queries, keyed)


def draw_query_rows(key, part):
    return paired_rows(key)[0].astype(jnp.bfloat16)


def draw_key_rows(key, part):
    return paired_rows(key)[1].astype(jnp.bfloat16)


def routing_draw(key):
    base = jax.random.fold_in(key, 29)
    hot_key, count_key, block_key = jax.random.split(base, 3)
    groups = N_SEQ * N_REP
    blocks = SEQS * groups
    hot = jax.random.randint(hot_key, (N_SEQ, N_REP), 0, EXPERTS).astype(jnp.int32)
    hot_count = jax.random.randint(count_key, (blocks,), CAP + 1, HOT_CAP + 1).astype(jnp.int32)
    hot_count = hot_count.at[0].set(CAP + 1).at[1].set(HOT_CAP)
    block_hot = jnp.tile(hot.reshape(groups), SEQS)

    def one_block(single_key, hot_id, count):
        order_key, spot_key = jax.random.split(single_key)
        shuffled = jax.random.permutation(order_key, EXPERTS).astype(jnp.int32)
        ranking = jnp.where(shuffled == hot_id, EXPERTS, jnp.arange(EXPERTS, dtype=jnp.int32))
        others = shuffled[jnp.argsort(ranking)]
        places = jnp.arange(TOK_DEV, dtype=jnp.int32)
        cold_place = places - count
        cycled = 1 + (cold_place - CAP) % (EXPERTS - 2)
        pick = jnp.where(places < count, EXPERTS - 1, jnp.where(cold_place < CAP, 0, cycled))
        named = others[pick]
        spots = jax.random.permutation(spot_key, TOK_DEV)
        return named[spots].astype(jnp.int32)
    routed = jax.vmap(one_block)(jax.random.split(block_key, blocks), block_hot, hot_count)
    return routed.reshape(SEQS, SEQ_LEN, 1)


def draw_expert_choice(key, part):
    return routing_draw(key)


def levels(stream_key, dims, pieces, least, high):
    loudness, own = 1.0, jax.random.fold_in(stream_key, 6)
    for position, parts in pieces:
        steps = jnp.exp(jax.random.uniform(jax.random.fold_in(own, position), (parts,), jnp.float32, least / len(pieces), high / len(pieces)))
        loudness = loudness * jnp.repeat(steps, dims[position] // parts).reshape([-1 if axis == position else 1 for axis in range(len(dims))])
    return loudness


def split_up(amount, total, bound, lean):
    portions = [(1 << 20) // math.isqrt(grade ** lean) + 1 for grade in range(2, amount + 1)]
    rest, holding = total - bound - (amount - 1), [1] * (amount - 1)
    while rest > 0:
        candidates = [i for i in range(amount - 1) if holding[i] < bound]
        pool, left = sum([portions[i] for i in candidates]), rest
        for i in candidates:
            more = min(bound - holding[i], max(1, left * portions[i] // pool), rest)
            holding[i] = holding[i] + more
            rest = rest - more
    return np.array([bound] + holding)


def ragged(own_key, number_of, total, bound, skew):
    if number_of == 2:
        one = jax.random.randint(own_key, (), max(1, total - bound), min(bound, total - 1) + 1)
        return jnp.stack([one, total - one])
    tallies = jnp.asarray(split_up(number_of, total, bound, skew), jnp.int32)
    pairs = (number_of - 1) // 2
    source_of, taker = tallies[1:1 + 2 * pairs:2], tallies[2:2 + 2 * pairs:2]
    margin = jnp.minimum(source_of - 1, bound - taker)
    moved = jax.random.randint(jax.random.fold_in(own_key, 1), (pairs,), 0, 1 << 20) % (margin + 1)
    tallies = tallies.at[1:1 + 2 * pairs:2].set(source_of - moved).at[2:2 + 2 * pairs:2].set(taker + moved)
    return tallies[jax.random.permutation(jax.random.fold_in(own_key, 2), number_of)]


def gaussian(own_key, dims, spread, most, cuts=(), held_as=jnp.bfloat16):
    level = levels(own_key, dims, cuts, -0.22, 0.18) if cuts else 1.0
    drawn = jax.random.normal(own_key, dims, jnp.float32) * spread * level
    return jnp.minimum(jnp.maximum(drawn, -most), most).astype(held_as)


def setup_inputs(seed: int = 0) -> dict:
    key_list = jax.random.split(jax.random.key(seed), 12)
    query_rows = draw_query_rows(jax.random.fold_in(key_list[11], 71), 0)
    key_rows = draw_key_rows(jax.random.fold_in(key_list[11], 71), 0)
    value_rows = gaussian(key_list[2], (SEQS, SEQ_LEN, D), 1.0, 6.0, ((0, 48), (1, 16)))
    doc_lengths = jax.vmap(lambda own: ragged(own, DOCS, SEQ_LEN, SEQ_LEN // 2, 2))(jax.random.split(key_list[3], SEQS)).reshape((SEQS, DOCS)).astype(jnp.int32)
    residual = gaussian(key_list[4], (SEQS, SEQ_LEN, D), 1.0, 6.0, ((0, 48), (1, 16)))
    out_proj = gaussian(key_list[5], (D, D), D ** -0.5, 0.25)
    router = gaussian(key_list[6], (D, EXPERTS), (D // 4) ** -0.5, 0.5)
    expert_choice = draw_expert_choice(jax.random.fold_in(key_list[11], 71), 0)
    weight_in = gaussian(key_list[8], (EXPERTS, D, FF), D ** -0.5, 0.25, ((0, 48),))
    weight_out = gaussian(key_list[9], (EXPERTS, FF, D), (FF // 4) ** -0.5, 0.5, ((0, 48),))
    grad_out = gaussian(key_list[10], (SEQS, SEQ_LEN, D), 1.0, 6.0, ((0, 48), (1, 16)))
    return dict(query_rows=query_rows, key_rows=key_rows, value_rows=value_rows, doc_lengths=doc_lengths, residual=residual, out_proj=out_proj, router=router, expert_choice=expert_choice, weight_in=weight_in, weight_out=weight_out, grad_out=grad_out)


norm_eps = 1e-06
masked_score = -1e+30
row_block = 512

def document_ids(lengths, positions):
    boundaries = jnp.cumsum(lengths).astype(jnp.int32)
    return lax.optimization_barrier(jnp.sum((positions[:, None] >= boundaries[None, :-1]).astype(jnp.int32), axis=1)).astype(jnp.int32)

def expert_pass(token_rows, grad_rows, weight_up, weight_down):
    hidden_pre = jnp.dot(token_rows, weight_up, preferred_element_type=jnp.float32)
    sigmoid_pre = jax.nn.sigmoid(hidden_pre)
    activated = (hidden_pre * sigmoid_pre).astype(jnp.bfloat16)
    produced = jnp.dot(activated, weight_down, preferred_element_type=jnp.float32).astype(jnp.bfloat16)
    act_grad = jnp.dot(grad_rows, weight_down.T, preferred_element_type=jnp.float32)
    pre_grad = (act_grad * sigmoid_pre * (1.0 + hidden_pre * (1.0 - sigmoid_pre))).astype(jnp.bfloat16)
    token_grad = jnp.dot(pre_grad, weight_up.T, preferred_element_type=jnp.float32).astype(jnp.bfloat16)
    up_grad = jnp.dot(token_rows.T, pre_grad, preferred_element_type=jnp.float32)
    down_grad = jnp.dot(activated.T, grad_rows, preferred_element_type=jnp.float32)
    return (produced, token_grad, up_grad, down_grad)

def attend_sequence(operands):
    queries, keyed, valued, lengths = operands
    positions = jnp.arange(SEQ_LEN, dtype=jnp.int32)
    docs = document_ids(lengths, positions)
    query_heads = queries.reshape(SEQ_LEN, H, HD).astype(jnp.float32)
    key_heads = keyed.reshape(SEQ_LEN, H, HD).astype(jnp.float32)
    value_heads = valued.reshape(SEQ_LEN, H, HD).astype(jnp.float32)
    scores = jnp.einsum('qhd,khd->hqk', query_heads, key_heads) * (1.0 / math.sqrt(HD))
    visible = (positions[None, :] <= positions[:, None]) & (docs[None, :] == docs[:, None])
    scores = jnp.where(visible[None], scores, masked_score)
    highest = lax.optimization_barrier(jnp.max(scores, axis=2, keepdims=True))
    weights = jnp.where(visible[None], jnp.exp(scores - highest), 0.0)
    totals = lax.optimization_barrier(jnp.sum(weights, axis=2))
    rounded = lax.optimization_barrier(weights.astype(jnp.bfloat16))
    summed = jnp.einsum('hqk,khd->hqd', rounded.astype(jnp.float32), value_heads)
    result = summed / totals[:, :, None]
    return result.transpose(1, 0, 2).reshape(SEQ_LEN, D).astype(jnp.bfloat16)

def reference(query_rows, key_rows, value_rows, doc_lengths, residual, out_proj, router, expert_choice, weight_in, weight_out, grad_out):
    attended = lax.map(attend_sequence, (query_rows, key_rows, value_rows, doc_lengths))
    token_total = SEQS * SEQ_LEN
    mixed = (residual.reshape(token_total, D).astype(jnp.float32) + jnp.dot(attended.reshape(token_total, D), out_proj, preferred_element_type=jnp.float32)).astype(jnp.bfloat16)
    mixed_f = mixed.astype(jnp.float32)
    inv_rms = lax.rsqrt(lax.optimization_barrier(jnp.mean(mixed_f * mixed_f, axis=1, keepdims=True)) + norm_eps)
    normed = (mixed_f * inv_rms).astype(jnp.bfloat16)
    chosen = expert_choice.reshape(token_total).astype(jnp.int32)
    logits = jnp.dot(normed, router, preferred_element_type=jnp.float32)
    gate_value = jax.nn.sigmoid(jnp.take_along_axis(logits, chosen[:, None], axis=1)[:, 0])
    grad_rows = grad_out.reshape(token_total, D)
    scaled_grad = (gate_value[:, None] * grad_rows.astype(jnp.float32)).astype(jnp.bfloat16)
    ordering = jnp.argsort(chosen, stable=True).astype(jnp.int32)
    counts = jnp.zeros((EXPERTS,), jnp.int32).at[chosen].add(1).astype(jnp.int32)
    begins = (jnp.cumsum(counts) - counts).astype(jnp.int32)
    sorted_rows = jnp.concatenate([normed[ordering], jnp.zeros((row_block, D), jnp.bfloat16)], axis=0)
    sorted_grads = jnp.concatenate([scaled_grad[ordering], jnp.zeros((row_block, D), jnp.bfloat16)], axis=0)

    def expert_loop(expert_index, carry):
        made, grads_back, up_all, down_all = carry
        begin_row = begins[expert_index].astype(jnp.int32)
        count = counts[expert_index].astype(jnp.int32)
        weight_up = weight_in[expert_index]
        weight_down = weight_out[expert_index]

        def block_loop(block_index, inner):
            made_in, back_in, up_acc, down_acc = inner
            first = (begin_row + block_index * row_block).astype(jnp.int32)
            local = (block_index * row_block + jnp.arange(row_block, dtype=jnp.int32)).astype(jnp.int32)
            usable = (local < count)[:, None]
            rows_in = jnp.where(usable, lax.dynamic_slice_in_dim(sorted_rows, first, row_block, 0), jnp.zeros((), jnp.bfloat16))
            grads_in = jnp.where(usable, lax.dynamic_slice_in_dim(sorted_grads, first, row_block, 0), jnp.zeros((), jnp.bfloat16))
            produced, token_grad, up_grad, down_grad = expert_pass(rows_in, grads_in, weight_up, weight_down)
            old_made = lax.dynamic_slice_in_dim(made_in, first, row_block, 0)
            old_back = lax.dynamic_slice_in_dim(back_in, first, row_block, 0)
            made_in = lax.dynamic_update_slice_in_dim(made_in, jnp.where(usable, produced, old_made), first, 0)
            back_in = lax.dynamic_update_slice_in_dim(back_in, jnp.where(usable, token_grad, old_back), first, 0)
            return (made_in, back_in, up_acc + up_grad, down_acc + down_grad)
        block_count = ((count + row_block - 1) // row_block).astype(jnp.int32)
        start_state = (made, grads_back, jnp.zeros((D, FF), jnp.float32), jnp.zeros((FF, D), jnp.float32))
        made, grads_back, up_acc, down_acc = lax.fori_loop(jnp.int32(0), block_count, block_loop, start_state)
        up_all = lax.dynamic_update_index_in_dim(up_all, up_acc, expert_index, 0)
        down_all = lax.dynamic_update_index_in_dim(down_all, down_acc, expert_index, 0)
        return (made, grads_back, up_all, down_all)
    start_all = (jnp.zeros((token_total + row_block, D), jnp.bfloat16), jnp.zeros((token_total + row_block, D), jnp.bfloat16), jnp.zeros((EXPERTS, D, FF), jnp.float32), jnp.zeros((EXPERTS, FF, D), jnp.float32))
    made, grads_back, grad_weight_in, grad_weight_out = lax.fori_loop(jnp.int32(0), jnp.int32(EXPERTS), expert_loop, start_all)
    expert_result = jnp.zeros((token_total, D), jnp.bfloat16).at[ordering].set(made[:token_total])
    normed_grad = jnp.zeros((token_total, D), jnp.bfloat16).at[ordering].set(grads_back[:token_total])
    result_f = expert_result.astype(jnp.float32)
    layer_out = (mixed_f + gate_value[:, None] * result_f).astype(jnp.bfloat16)
    gate_grad = lax.optimization_barrier(jnp.sum(grad_rows.astype(jnp.float32) * result_f, axis=1))
    logit_grad = gate_grad * gate_value * (1.0 - gate_value)
    router_cols = router[:, chosen].T.astype(jnp.float32)
    total_grad = normed_grad.astype(jnp.float32) + logit_grad[:, None] * router_cols
    mean_term = lax.optimization_barrier(jnp.mean(total_grad * mixed_f, axis=1, keepdims=True))
    input_grad = inv_rms * total_grad - mixed_f * inv_rms * inv_rms * inv_rms * mean_term
    grad_mixed = (grad_rows.astype(jnp.float32) + input_grad).astype(jnp.bfloat16)
    return (layer_out.reshape(SEQS, SEQ_LEN, D), grad_mixed.reshape(SEQS, SEQ_LEN, D), grad_weight_in, grad_weight_out)
```

```python
import functools
import math

import jax
import jax.numpy as jnp
from jax import lax
from jax.experimental import pallas as pl
from jax.experimental.pallas import tpu as pltpu
from jax.sharding import PartitionSpec as P

D = 512
H = 16
HD = 32
FF = 512
T = 128
EXPERTS = 48
SLOTS = 16
WINDOW = 1024
norm_eps = 1e-06
masked_score = -1e30
F32 = jnp.float32
BF16 = jnp.bfloat16
VMEM = pl.BlockSpec(memory_space=pltpu.VMEM)


def attention_body(blocks, start_ref, heads_ref, out_ref, q_all, k_all, v_all):
    seq = blocks * T
    for b in range(blocks):
        cols = pl.ds(b * T, T)
        q_all[:, cols] = heads_ref[b, 0:HD, :]
        v_all[:, cols] = heads_ref[b, 2 * HD : 3 * HD, :]
        k_all[cols, :] = heads_ref[b, HD : 2 * HD, :].astype(F32).T.astype(BF16)
    scale = math.log2(math.e) / math.sqrt(HD)
    chunk = 256
    for c in range(seq // chunk):
        first_q = c * chunk
        first_k = max(0, first_q - WINDOW)
        span = first_q + chunk - first_k
        queries = pl.ds(first_q, chunk)
        scores = jnp.dot(
            k_all[pl.ds(first_k, span), :], q_all[:, queries], preferred_element_type=F32
        )
        key_pos = lax.broadcasted_iota(jnp.int32, (span, chunk), 0) + first_k
        query_pos = lax.broadcasted_iota(jnp.int32, (span, chunk), 1) + first_q
        visible = (key_pos >= start_ref[:, queries]) & (key_pos <= query_pos)
        scores = jnp.where(visible, scores, masked_score)
        top = jnp.max(scores, axis=0, keepdims=True)
        weights = jnp.exp2((scores - top) * scale)
        totals = jnp.sum(weights, axis=0, keepdims=True)
        result = jnp.dot(
            v_all[:, pl.ds(first_k, span)], weights.astype(BF16), preferred_element_type=F32
        )
        result = (result / totals).astype(BF16)
        for j in range(chunk // T):
            out_ref[c * (chunk // T) + j] = result[:, j * T : (j + 1) * T]


def attention(heads, start):
    blocks = heads.shape[0]
    seq = blocks * T
    return pl.pallas_call(
        functools.partial(attention_body, blocks),
        out_shape=jax.ShapeDtypeStruct((blocks, HD, T), BF16),
        in_specs=[VMEM, VMEM],
        out_specs=VMEM,
        scratch_shapes=[
            pltpu.VMEM((HD, seq), BF16),
            pltpu.VMEM((seq, HD), BF16),
            pltpu.VMEM((HD, seq), BF16),
        ],
        cost_estimate=pl.CostEstimate(flops=300000000, bytes_accessed=600000, transcendentals=2000000),
        name="attention",
    )(start, heads)


def slots_row(chosen_row, experts, slots):
    ids = lax.broadcasted_iota(jnp.int32, (experts, T), 0)
    hits = chosen_row == ids
    before = lax.broadcasted_iota(jnp.int32, (T, T), 0) < lax.broadcasted_iota(
        jnp.int32, (T, T), 1
    )
    ranks = jnp.dot(
        hits.astype(F32).astype(BF16), before.astype(F32).astype(BF16), preferred_element_type=F32
    )
    rank = jnp.sum(jnp.where(hits, ranks, 0.0), axis=0, keepdims=True)
    return chosen_row * slots + rank.astype(jnp.int32)


def slots_column(hits, chosen_col, slots):
    before = lax.broadcasted_iota(jnp.int32, (T, T), 1) < lax.broadcasted_iota(
        jnp.int32, (T, T), 0
    )
    ranks = jnp.dot(
        before.astype(F32).astype(BF16), hits.astype(F32).astype(BF16), preferred_element_type=F32
    )
    rank = jnp.sum(jnp.where(hits, ranks, 0.0), axis=1, keepdims=True)
    return chosen_col * slots + rank.astype(jnp.int32)


def mix_body(
    experts, att_ref, residual_ref, proj_ref, router_ref, row_ref, col_ref, grad_ref,
    mixed_ref, stats_ref, send_ref,
):
    attended = att_ref[...].astype(F32).T.astype(BF16)
    mixed = (
        residual_ref[...].astype(F32)
        + jnp.dot(attended, proj_ref[...], preferred_element_type=F32)
    ).astype(BF16)
    mixed_ref[...] = mixed
    mixed_f = mixed.astype(F32)
    inv_rms = lax.rsqrt(jnp.mean(mixed_f * mixed_f, axis=1, keepdims=True) + norm_eps)
    normed = (mixed_f * inv_rms).astype(BF16)
    logits = jnp.dot(normed, router_ref[...], preferred_element_type=F32)
    hits = col_ref[...] == lax.broadcasted_iota(jnp.int32, (T, experts), 1)
    gate = jax.nn.sigmoid(jnp.sum(jnp.where(hits, logits, 0.0), axis=1, keepdims=True))
    scaled = (gate * grad_ref[...].astype(F32)).astype(BF16)
    stats_ref[...] = jnp.concatenate(
        [jnp.broadcast_to(inv_rms, (T, T)), jnp.broadcast_to(gate, (T, T))], axis=1
    )
    slot = slots_row(row_ref[...], experts, SLOTS)
    place = lax.broadcasted_iota(jnp.int32, (experts * SLOTS, T), 0) == slot
    place = place.astype(F32).astype(BF16)
    send_ref[:, 0:D] = jnp.dot(place, normed, preferred_element_type=F32).astype(BF16)
    send_ref[:, D : 2 * D] = jnp.dot(place, scaled, preferred_element_type=F32).astype(BF16)


def final_body(
    experts, back_ref, mixed_ref, stats_ref, router_ref, col_ref, grad_ref, out_ref, grad_mixed_ref
):
    chosen = col_ref[...]
    hits = chosen == lax.broadcasted_iota(jnp.int32, (T, experts), 1)
    slot = slots_column(hits, chosen, SLOTS)
    pick = lax.broadcasted_iota(jnp.int32, (T, experts * SLOTS), 1) == slot
    pick = pick.astype(F32).astype(BF16)
    result_f = jnp.dot(pick, back_ref[:, 0:D], preferred_element_type=F32)
    normed_grad = jnp.dot(pick, back_ref[:, D : 2 * D], preferred_element_type=F32)
    mixed_f = mixed_ref[...].astype(F32)
    inv_rms = stats_ref[:, 0:1]
    gate = stats_ref[:, T : T + 1]
    grad_f = grad_ref[...].astype(F32)
    out_ref[...] = (mixed_f + gate * result_f).astype(BF16)
    gate_grad = jnp.sum(grad_f * result_f, axis=1, keepdims=True)
    logit_grad = gate_grad * gate * (1.0 - gate)
    router_cols = lax.dot_general(
        hits.astype(F32).astype(BF16), router_ref[...], (((1,), (1,)), ((), ())),
        preferred_element_type=F32,
    )
    total_grad = normed_grad + logit_grad * router_cols
    mean_term = jnp.mean(total_grad * mixed_f, axis=1, keepdims=True)
    input_grad = inv_rms * total_grad - mixed_f * inv_rms * inv_rms * inv_rms * mean_term
    grad_mixed_ref[...] = (grad_f + input_grad).astype(BF16)


def expert_body(rows_ref, up_ref, down_ref, back_ref, grads_ref, act_ref, pre_ref):
    up = up_ref[...]
    down = down_ref[...]
    rows = rows_ref.shape[0]
    step = 256
    contract_last = (((1,), (1,)), ((), ()))
    contract_first = (((0,), (0,)), ((), ()))

    def block(i, carry):
        here = pl.ds(pl.multiple_of(i * step, step), step)
        tokens = rows_ref[here, 0:D]
        grads = rows_ref[here, D : 2 * D]
        pre = jnp.dot(tokens, up, preferred_element_type=F32)
        sig = jax.nn.sigmoid(pre)
        activated = (pre * sig).astype(BF16)
        back_ref[here, 0:D] = jnp.dot(activated, down, preferred_element_type=F32).astype(BF16)
        act_grad = lax.dot_general(grads, down, contract_last, preferred_element_type=F32)
        pre_grad = (act_grad * sig * (1.0 + pre * (1.0 - sig))).astype(BF16)
        back_ref[here, D : 2 * D] = lax.dot_general(
            pre_grad, up, contract_last, preferred_element_type=F32
        ).astype(BF16)
        act_ref[here, :] = activated
        pre_ref[here, :] = pre_grad
        return carry

    lax.fori_loop(0, rows // step, block, 0)
    grad_up = lax.dot_general(
        rows_ref[:, 0:D], pre_ref[...], contract_first, preferred_element_type=F32
    )
    grads_ref[:, 0:FF] = grad_up.astype(BF16)
    grad_down = lax.dot_general(
        act_ref[...], rows_ref[:, D : 2 * D], contract_first, preferred_element_type=F32
    )
    grads_ref[:, FF : FF + D] = grad_down.astype(BF16)


def sum_body(parts, got_ref, in_ref, out_ref):
    total = got_ref[0].astype(F32)
    for p in range(1, parts):
        total = total + got_ref[p].astype(F32)
    in_ref[...] = total[:, 0:FF]
    out_ref[...] = total[:, FF : FF + D]


def local(
    query_rows, key_rows, value_rows, doc_lengths, residual, out_proj, router, expert_choice,
    weight_in, weight_out, grad_out,
):
    ranks = lax.axis_size(("seq", "rep"))
    experts = router.shape[1]
    seq = ranks * T
    group = ("seq", "rep")
    heads = jnp.concatenate(
        [
            query_rows[0].T.reshape(H, HD, T),
            key_rows[0].T.reshape(H, HD, T),
            value_rows[0].T.reshape(H, HD, T),
        ],
        axis=1,
    )
    heads = lax.all_to_all(heads, group, split_axis=0, concat_axis=0, tiled=True)
    boundaries = jnp.cumsum(doc_lengths[0])[:-1]
    positions = jnp.arange(seq, dtype=jnp.int32)
    start = jnp.max(
        jnp.where(positions[None, :] >= boundaries[:, None], boundaries[:, None], 0),
        axis=0,
        keepdims=True,
    )
    attended = attention(heads, start)
    attended = lax.all_to_all(attended, group, split_axis=0, concat_axis=0, tiled=True)
    chosen_col = expert_choice[0]
    chosen_row = chosen_col.reshape(1, T)
    grad_rows = grad_out[0]
    mixed, stats, send = pl.pallas_call(
        functools.partial(mix_body, experts),
        out_shape=(
            jax.ShapeDtypeStruct((T, D), BF16),
            jax.ShapeDtypeStruct((T, 2 * T), F32),
            jax.ShapeDtypeStruct((experts * SLOTS, 2 * D), BF16),
        ),
        in_specs=[VMEM] * 7,
        out_specs=(VMEM,) * 3,
        name="mix",
    )(attended.reshape(D, T), residual[0], out_proj, router, chosen_row, chosen_col, grad_rows)
    got = lax.all_to_all(
        send.reshape(experts, SLOTS, 2 * D), "expert", split_axis=0, concat_axis=0, tiled=True
    )
    back, grads = pl.pallas_call(
        expert_body,
        out_shape=(
            jax.ShapeDtypeStruct((experts * SLOTS, 2 * D), BF16),
            jax.ShapeDtypeStruct((D, FF + D), BF16),
        ),
        in_specs=[VMEM] * 3,
        out_specs=(VMEM,) * 2,
        scratch_shapes=[
            pltpu.VMEM((experts * SLOTS, FF), BF16),
            pltpu.VMEM((experts * SLOTS, FF), BF16),
        ],
        cost_estimate=pl.CostEstimate(flops=2400000000, bytes_accessed=5000000, transcendentals=400000),
        name="expert",
    )(got.reshape(experts * SLOTS, 2 * D), weight_in[0], weight_out[0])
    back = lax.all_to_all(
        back.reshape(experts, SLOTS, 2 * D), "expert", split_axis=0, concat_axis=0, tiled=True
    )
    shares = lax.all_to_all(
        grads.reshape(ranks, D // ranks, FF + D), group, split_axis=0, concat_axis=0, tiled=True
    )
    share_in, share_out = pl.pallas_call(
        functools.partial(sum_body, ranks),
        out_shape=(jax.ShapeDtypeStruct((D // ranks, FF), F32),) * 2,
        in_specs=[VMEM],
        out_specs=(VMEM,) * 2,
        name="grad_sum",
    )(shares)
    layer_out, grad_mixed = pl.pallas_call(
        functools.partial(final_body, experts),
        out_shape=(jax.ShapeDtypeStruct((T, D), BF16),) * 2,
        in_specs=[VMEM] * 6,
        out_specs=(VMEM,) * 2,
        name="final",
    )(back.reshape(experts * SLOTS, 2 * D), mixed, stats, router, chosen_col, grad_rows)
    return (layer_out[None], grad_mixed[None], share_in[None], share_out[None])


def solution(mesh):
    rows = P("expert", ("seq", "rep"), None)
    weights = P("expert", None, None)
    in_specs = (
        rows, rows, rows, P("expert", None), rows, P(), P(), rows, weights, weights, rows,
    )
    return jax.shard_map(
        local, mesh=mesh, in_specs=in_specs, out_specs=(rows,) * 4, check_vma=False
    )
```

```python
import functools
import math

import jax
import jax.numpy as jnp
from jax import lax
from jax.experimental import pallas as pl
from jax.experimental.pallas import tpu as pltpu
from jax.sharding import PartitionSpec as P

D = 512
H = 16
HD = 32
FF = 512
T = 128
EXPERTS = 48
SLOTS = 16
WINDOW = 1024
CHUNK = 256
MESH = pl.DeviceIdType.MESH
norm_eps = 1e-06
masked_score = -1e30
F32 = jnp.float32
BF16 = jnp.bfloat16
VMEM = pl.BlockSpec(memory_space=pltpu.VMEM)


def group_device(rank, reps):
    return {"seq": rank // reps, "rep": lax.rem(rank, reps)}


def attend_chunk(c, start, q_all, k_all, v_all):
    scale = math.log2(math.e) / math.sqrt(HD)
    first_q = c * CHUNK
    first_k = max(0, first_q - WINDOW)
    span = first_q + CHUNK - first_k
    queries = pl.ds(first_q, CHUNK)
    scores = jnp.dot(
        k_all[pl.ds(first_k, span), :], q_all[:, queries], preferred_element_type=F32
    )
    key_pos = lax.broadcasted_iota(jnp.int32, (span, CHUNK), 0) + first_k
    query_pos = lax.broadcasted_iota(jnp.int32, (span, CHUNK), 1) + first_q
    visible = (key_pos >= start) & (key_pos <= query_pos)
    scores = jnp.where(visible, scores, masked_score)
    top = jnp.max(scores, axis=0, keepdims=True)
    weights = jnp.exp2((scores - top) * scale)
    totals = jnp.sum(weights, axis=0, keepdims=True)
    result = jnp.dot(
        v_all[:, pl.ds(first_k, span)], weights.astype(BF16), preferred_element_type=F32
    )
    return (result / totals).astype(BF16)


def attend_body(
    blocks, reps, experts, lengths_ref, query_ref, key_ref, value_ref, residual_ref, proj_ref,
    router_ref, row_ref, col_ref, grad_ref, mixed_ref, stats_ref, send_ref,
    heads, got, result, att, q_all, k_all, v_all,
    send_sem, recv_sem, back_send_sem, back_recv_sem,
):
    me = lax.axis_index("seq") * reps + lax.axis_index("rep")
    barrier = pltpu.get_barrier_semaphore()

    def greet(k, carry):
        pl.semaphore_signal(
            barrier, inc=1, device_id=group_device(lax.rem(me + k, blocks), reps),
            device_id_type=MESH,
        )
        return carry

    lax.fori_loop(1, blocks, greet, 0)
    for i, ref in enumerate((query_ref, key_ref, value_ref)):
        flipped = ref[...].astype(F32).T.astype(BF16)
        for h in range(blocks):
            heads[h, i * HD : (i + 1) * HD, :] = flipped[h * HD : (h + 1) * HD]
    starts = []
    for c in range(blocks * T // CHUNK):
        pos = lax.broadcasted_iota(jnp.int32, (1, CHUNK), 1) + c * CHUNK
        edge = jnp.int32(0)
        start = jnp.zeros((1, CHUNK), jnp.int32)
        for d in range(lengths_ref.shape[1] - 1):
            edge = edge + lengths_ref[0, d]
            start = jnp.where(pos >= edge, edge, start)
        starts.append(start)
    pl.semaphore_wait(barrier, blocks - 1)

    def outgoing(k):
        to = lax.rem(me + k, blocks)
        return pltpu.make_async_remote_copy(
            src_ref=heads.at[to], dst_ref=got.at[me], send_sem=send_sem.at[to],
            recv_sem=recv_sem.at[me], device_id=group_device(to, reps), device_id_type=MESH,
        )

    def launch(k, carry):
        outgoing(k).start()
        return carry

    lax.fori_loop(1, blocks, launch, 0)
    got[me] = heads[me]

    def incoming(b):
        return pltpu.make_async_remote_copy(
            src_ref=heads.at[b], dst_ref=got.at[b], send_sem=send_sem.at[b],
            recv_sem=recv_sem.at[b], device_id=group_device(b, reps), device_id_type=MESH,
        )

    def returning(b):
        return pltpu.make_async_remote_copy(
            src_ref=result.at[b], dst_ref=att.at[me], send_sem=back_send_sem.at[b],
            recv_sem=back_recv_sem.at[me], device_id=group_device(b, reps), device_id_type=MESH,
        )

    per = CHUNK // T

    def give_back(c):
        for b in range(c * per, (c + 1) * per):

            @pl.when(me != b)
            def _():
                returning(b).start()

            @pl.when(me == b)
            def _():
                att[b] = result[b]

    chunks = blocks // per
    for c in range(chunks):
        for b in range(c * per, (c + 1) * per):

            @pl.when(me != b)
            def _():
                incoming(b).wait_recv()

            cols = pl.ds(b * T, T)
            q_all[:, cols] = got[b, 0:HD, :]
            v_all[:, cols] = got[b, 2 * HD : 3 * HD, :]
            k_all[cols, :] = got[b, HD : 2 * HD, :].astype(F32).T.astype(BF16)
        done = attend_chunk(c, starts[c], q_all, k_all, v_all)
        for j in range(per):
            result[c * per + j] = done[:, j * T : (j + 1) * T]
        if c:
            give_back(c - 1)
    slot = slots_row(row_ref[...], experts, SLOTS)
    place = lax.broadcasted_iota(jnp.int32, (experts * SLOTS, T), 0) == slot
    place = place.astype(F32).astype(BF16)
    give_back(chunks - 1)

    def arrived(k, carry):
        b = lax.rem(me + k, blocks)
        pltpu.make_async_remote_copy(
            src_ref=result.at[b], dst_ref=att.at[b], send_sem=back_send_sem.at[b],
            recv_sem=back_recv_sem.at[b], device_id=group_device(b, reps), device_id_type=MESH,
        ).wait_recv()
        return carry

    lax.fori_loop(1, blocks, arrived, 0)
    attended = att[...].reshape(D, T).astype(F32).T.astype(BF16)
    mixed = (
        residual_ref[...].astype(F32)
        + jnp.dot(attended, proj_ref[...], preferred_element_type=F32)
    ).astype(BF16)
    mixed_ref[...] = mixed
    mixed_f = mixed.astype(F32)
    inv_rms = lax.rsqrt(jnp.mean(mixed_f * mixed_f, axis=1, keepdims=True) + norm_eps)
    normed = (mixed_f * inv_rms).astype(BF16)
    logits = jnp.dot(normed, router_ref[...], preferred_element_type=F32)
    hits = col_ref[...] == lax.broadcasted_iota(jnp.int32, (T, experts), 1)
    gate = jax.nn.sigmoid(jnp.sum(jnp.where(hits, logits, 0.0), axis=1, keepdims=True))
    scaled = (gate * grad_ref[...].astype(F32)).astype(BF16)
    stats_ref[...] = jnp.concatenate(
        [jnp.broadcast_to(inv_rms, (T, T)), jnp.broadcast_to(gate, (T, T))], axis=1
    )
    send_ref[:, 0:D] = jnp.dot(place, normed, preferred_element_type=F32).astype(BF16)
    send_ref[:, D : 2 * D] = jnp.dot(place, scaled, preferred_element_type=F32).astype(BF16)

    def finish(k, carry):
        outgoing(k).wait_send()
        returning(lax.rem(me + k, blocks)).wait_send()
        return carry

    lax.fori_loop(1, blocks, finish, 0)


def slots_row(chosen_row, experts, slots):
    ids = lax.broadcasted_iota(jnp.int32, (experts, T), 0)
    hits = chosen_row == ids
    before = lax.broadcasted_iota(jnp.int32, (T, T), 0) < lax.broadcasted_iota(
        jnp.int32, (T, T), 1
    )
    ranks = jnp.dot(
        hits.astype(F32).astype(BF16), before.astype(F32).astype(BF16), preferred_element_type=F32
    )
    rank = jnp.sum(jnp.where(hits, ranks, 0.0), axis=0, keepdims=True)
    return chosen_row * slots + rank.astype(jnp.int32)


def slots_column(hits, chosen_col, slots):
    before = lax.broadcasted_iota(jnp.int32, (T, T), 1) < lax.broadcasted_iota(
        jnp.int32, (T, T), 0
    )
    ranks = jnp.dot(
        before.astype(F32).astype(BF16), hits.astype(F32).astype(BF16), preferred_element_type=F32
    )
    rank = jnp.sum(jnp.where(hits, ranks, 0.0), axis=1, keepdims=True)
    return chosen_col * slots + rank.astype(jnp.int32)


def final_body(
    experts, back_ref, mixed_ref, stats_ref, router_ref, col_ref, grad_ref, out_ref, grad_mixed_ref
):
    chosen = col_ref[...]
    hits = chosen == lax.broadcasted_iota(jnp.int32, (T, experts), 1)
    slot = slots_column(hits, chosen, SLOTS)
    pick = lax.broadcasted_iota(jnp.int32, (T, experts * SLOTS), 1) == slot
    pick = pick.astype(F32).astype(BF16)
    result_f = jnp.dot(pick, back_ref[:, 0:D], preferred_element_type=F32)
    normed_grad = jnp.dot(pick, back_ref[:, D : 2 * D], preferred_element_type=F32)
    mixed_f = mixed_ref[...].astype(F32)
    inv_rms = stats_ref[:, 0:1]
    gate = stats_ref[:, T : T + 1]
    grad_f = grad_ref[...].astype(F32)
    out_ref[...] = (mixed_f + gate * result_f).astype(BF16)
    gate_grad = jnp.sum(grad_f * result_f, axis=1, keepdims=True)
    logit_grad = gate_grad * gate * (1.0 - gate)
    router_cols = lax.dot_general(
        hits.astype(F32).astype(BF16), router_ref[...], (((1,), (1,)), ((), ())),
        preferred_element_type=F32,
    )
    total_grad = normed_grad + logit_grad * router_cols
    mean_term = jnp.mean(total_grad * mixed_f, axis=1, keepdims=True)
    input_grad = inv_rms * total_grad - mixed_f * inv_rms * inv_rms * inv_rms * mean_term
    grad_mixed_ref[...] = (grad_f + input_grad).astype(BF16)


def expert_body(rows_ref, up_ref, down_ref, back_ref, grads_ref, act_ref, pre_ref):
    up = up_ref[...]
    down = down_ref[...]
    rows = rows_ref.shape[0]
    step = 256
    contract_last = (((1,), (1,)), ((), ()))
    contract_first = (((0,), (0,)), ((), ()))

    def block(i, carry):
        here = pl.ds(pl.multiple_of(i * step, step), step)
        tokens = rows_ref[here, 0:D]
        grads = rows_ref[here, D : 2 * D]
        pre = jnp.dot(tokens, up, preferred_element_type=F32)
        sig = jax.nn.sigmoid(pre)
        activated = (pre * sig).astype(BF16)
        back_ref[here, 0:D] = jnp.dot(activated, down, preferred_element_type=F32).astype(BF16)
        act_grad = lax.dot_general(grads, down, contract_last, preferred_element_type=F32)
        pre_grad = (act_grad * sig * (1.0 + pre * (1.0 - sig))).astype(BF16)
        back_ref[here, D : 2 * D] = lax.dot_general(
            pre_grad, up, contract_last, preferred_element_type=F32
        ).astype(BF16)
        act_ref[here, :] = activated
        pre_ref[here, :] = pre_grad
        return carry

    lax.fori_loop(0, rows // step, block, 0)
    reps = grads_ref.shape[1]
    share = grads_ref.shape[3]
    grad_up = lax.dot_general(
        rows_ref[:, 0:D], pre_ref[...], contract_first, preferred_element_type=F32
    )
    grad_down = lax.dot_general(
        act_ref[...], rows_ref[:, D : 2 * D], contract_first, preferred_element_type=F32
    )
    for m, grad in enumerate((grad_up, grad_down)):
        for j in range(D // share):
            piece = grad[j * share : (j + 1) * share]
            grads_ref[m, j % reps, j // reps] = piece.astype(BF16)


def reduce_body(
    seqs, reps, grads_ref, in_ref, out_ref, got_x, part, got_z,
    x_send, x_recv, z_send, z_recv,
):
    my_seq = lax.axis_index("seq")
    my_rep = lax.axis_index("rep")
    barrier = pltpu.get_barrier_semaphore()
    for k in range(1, reps):
        pl.semaphore_signal(
            barrier, inc=1, device_id={"rep": lax.rem(my_rep + k, reps)}, device_id_type=MESH
        )
    for k in range(1, seqs):
        pl.semaphore_signal(
            barrier, inc=1, device_id={"seq": lax.rem(my_seq + k, seqs)}, device_id_type=MESH
        )
    pl.semaphore_wait(barrier, reps + seqs - 2)

    def along_x(m, k):
        to = lax.rem(my_rep + k, reps)
        return pltpu.make_async_remote_copy(
            src_ref=grads_ref.at[m, to], dst_ref=got_x.at[m, k - 1],
            send_sem=x_send.at[m, k - 1], recv_sem=x_recv.at[m, k - 1],
            device_id={"rep": to}, device_id_type=MESH,
        )

    def along_z(m, k):
        to = lax.rem(my_seq + k, seqs)
        return pltpu.make_async_remote_copy(
            src_ref=part.at[m, to], dst_ref=got_z.at[m, k - 1],
            send_sem=z_send.at[m, k - 1], recv_sem=z_recv.at[m, k - 1],
            device_id={"seq": to}, device_id_type=MESH,
        )

    for m in range(2):
        for k in range(1, reps):
            along_x(m, k).start()
    for m in range(2):
        for k in range(1, reps):
            along_x(m, k).wait_recv()
        for p in range(seqs):
            total = grads_ref[m, my_rep, p].astype(F32)
            for k in range(1, reps):
                total = total + got_x[m, k - 1, p].astype(F32)
            part[m, p] = total.astype(BF16)
        for k in range(1, seqs):
            along_z(m, k).start()
    for m, ref in enumerate((in_ref, out_ref)):
        for k in range(1, seqs):
            along_z(m, k).wait_recv()
        total = part[m, my_seq].astype(F32)
        for k in range(1, seqs):
            total = total + got_z[m, k - 1].astype(F32)
        ref[...] = total
    for m in range(2):
        for k in range(1, reps):
            along_x(m, k).wait_send()
        for k in range(1, seqs):
            along_z(m, k).wait_send()


def local(
    query_rows, key_rows, value_rows, doc_lengths, residual, out_proj, router, expert_choice,
    weight_in, weight_out, grad_out,
):
    seqs, reps = lax.axis_size("seq"), lax.axis_size("rep")
    ranks = seqs * reps
    share = D // ranks
    experts = router.shape[1]
    chosen_col = expert_choice[0]
    chosen_row = chosen_col.reshape(1, T)
    grad_rows = grad_out[0]
    mixed, stats, send = pl.pallas_call(
        functools.partial(attend_body, ranks, reps, experts),
        out_shape=(
            jax.ShapeDtypeStruct((T, D), BF16),
            jax.ShapeDtypeStruct((T, 2 * T), F32),
            jax.ShapeDtypeStruct((experts * SLOTS, 2 * D), BF16),
        ),
        in_specs=[pl.BlockSpec(memory_space=pltpu.SMEM)] + [VMEM] * 9,
        out_specs=(VMEM,) * 3,
        scratch_shapes=[
            pltpu.VMEM((ranks, 3 * HD, T), BF16),
            pltpu.VMEM((ranks, 3 * HD, T), BF16),
            pltpu.VMEM((ranks, HD, T), BF16),
            pltpu.VMEM((ranks, HD, T), BF16),
            pltpu.VMEM((HD, ranks * T), BF16),
            pltpu.VMEM((ranks * T, HD), BF16),
            pltpu.VMEM((HD, ranks * T), BF16),
        ]
        + [pltpu.SemaphoreType.DMA((ranks,))] * 4,
        compiler_params=pltpu.CompilerParams(collective_id=1, has_side_effects=True),
        cost_estimate=pl.CostEstimate(
            flops=400000000, bytes_accessed=4000000, transcendentals=2000000
        ),
        name="attend",
    )(
        doc_lengths, query_rows[0], key_rows[0], value_rows[0], residual[0], out_proj, router,
        chosen_row, chosen_col, grad_rows,
    )
    got = lax.all_to_all(
        send.reshape(experts, SLOTS, 2 * D), "expert", split_axis=0, concat_axis=0, tiled=True
    )
    back, grads = pl.pallas_call(
        expert_body,
        out_shape=(
            jax.ShapeDtypeStruct((experts * SLOTS, 2 * D), BF16),
            jax.ShapeDtypeStruct((2, reps, seqs, share, FF), BF16),
        ),
        in_specs=[VMEM] * 3,
        out_specs=(VMEM,) * 2,
        scratch_shapes=[
            pltpu.VMEM((experts * SLOTS, FF), BF16),
            pltpu.VMEM((experts * SLOTS, FF), BF16),
        ],
        cost_estimate=pl.CostEstimate(flops=2400000000, bytes_accessed=5000000, transcendentals=400000),
        name="expert",
    )(got.reshape(experts * SLOTS, 2 * D), weight_in[0], weight_out[0])
    back = lax.all_to_all(
        back.reshape(experts, SLOTS, 2 * D), "expert", split_axis=0, concat_axis=0, tiled=True
    )
    share_in, share_out = pl.pallas_call(
        functools.partial(reduce_body, seqs, reps),
        out_shape=(jax.ShapeDtypeStruct((share, FF), F32),) * 2,
        in_specs=[VMEM],
        out_specs=(VMEM,) * 2,
        scratch_shapes=[
            pltpu.VMEM((2, reps - 1, seqs, share, FF), BF16),
            pltpu.VMEM((2, seqs, share, FF), BF16),
            pltpu.VMEM((2, seqs - 1, share, FF), BF16),
            pltpu.SemaphoreType.DMA((2, reps - 1)),
            pltpu.SemaphoreType.DMA((2, reps - 1)),
            pltpu.SemaphoreType.DMA((2, seqs - 1)),
            pltpu.SemaphoreType.DMA((2, seqs - 1)),
        ],
        compiler_params=pltpu.CompilerParams(collective_id=2, has_side_effects=True),
        cost_estimate=pl.CostEstimate(flops=20000000, bytes_accessed=40000000, transcendentals=0),
        name="grad_reduce",
    )(grads)
    layer_out, grad_mixed = pl.pallas_call(
        functools.partial(final_body, experts),
        out_shape=(jax.ShapeDtypeStruct((T, D), BF16),) * 2,
        in_specs=[VMEM] * 6,
        out_specs=(VMEM,) * 2,
        name="final",
    )(back.reshape(experts * SLOTS, 2 * D), mixed, stats, router, chosen_col, grad_rows)
    return (layer_out[None], grad_mixed[None], share_in[None], share_out[None])


def solution(mesh):
    rows = P("expert", ("seq", "rep"), None)
    weights = P("expert", None, None)
    in_specs = (
        rows, rows, rows, P("expert", None), rows, P(), P(), rows, weights, weights, rows,
    )
    return jax.shard_map(
        local, mesh=mesh, in_specs=in_specs, out_specs=(rows,) * 4, check_vma=False
    )
```

```python
import functools
import math

import jax
import jax.numpy as jnp
from jax import lax
from jax.experimental import pallas as pl
from jax.experimental.pallas import tpu as pltpu
from jax.sharding import PartitionSpec as P

D = 512
H = 16
HD = 32
FF = 512
T = 128
EXPERTS = 48
CAP = 4
HOT = 16
PAIR = 2 * CAP
CORES = 2
DEPTH = 3
WINDOW = 1024
CHUNK = 256
MESH = pl.DeviceIdType.MESH
norm_eps = 1e-06
masked_score = -1e30
F32 = jnp.float32
BF16 = jnp.bfloat16
VMEM = pl.BlockSpec(memory_space=pltpu.VMEM)


def group_device(rank, reps):
    return {"seq": rank // reps, "rep": lax.rem(rank, reps)}


def attend_chunk(c, start, q_all, k_all, v_all):
    scale = math.log2(math.e) / math.sqrt(HD)
    first_q = c * CHUNK
    first_k = max(0, first_q - WINDOW)
    span = first_q + CHUNK - first_k
    queries = pl.ds(first_q, CHUNK)
    scores = jnp.dot(
        k_all[pl.ds(first_k, span), :], q_all[:, queries], preferred_element_type=F32
    )
    key_pos = lax.broadcasted_iota(jnp.int32, (span, CHUNK), 0) + first_k
    query_pos = lax.broadcasted_iota(jnp.int32, (span, CHUNK), 1) + first_q
    visible = (key_pos >= start) & (key_pos <= query_pos)
    scores = jnp.where(visible, scores, masked_score)
    top = jnp.max(scores, axis=0, keepdims=True)
    weights = jnp.exp2((scores - top) * scale)
    totals = jnp.sum(weights, axis=0, keepdims=True)
    result = jnp.dot(
        v_all[:, pl.ds(first_k, span)], weights.astype(BF16), preferred_element_type=F32
    )
    return (result / totals).astype(BF16)


def remote(src, dst, send_sem, recv_sem, device):
    return pltpu.make_async_remote_copy(
        src_ref=src, dst_ref=dst, send_sem=send_sem, recv_sem=recv_sem, device_id=device,
        device_id_type=MESH,
    )


def ones(mask):
    return mask.astype(F32).astype(BF16)


def step_body(
    seqs, reps, experts,
    lengths_ref, query_ref, key_ref, value_ref, residual_ref, proj_ref, router_ref, row_ref,
    grad_ref, up_hbm, down_hbm,
    out_ref, grad_mixed_ref, share_in_ref, share_out_ref,
    heads, got, result, att, q_all, k_all, v_all, up_ref, down_ref,
    cold_send, cold_got, made_send, made_got,
    hot_all, hot_res, core_got, y_send, y_got, z_send, z_got,
    act_ref, pre_ref, grads, got_x, part, got_zz,
    load_sem, send_sem, recv_sem, back_send_sem, back_recv_sem,
    cold_ssem, cold_rsem, made_ssem, made_rsem,
    hz_ssem, hz_rsem, ring_ssem, ring_rsem, hc_ssem, hc_rsem,
    core_ssem, core_rsem, y_ssem, y_rsem, z_ssem, z_rsem,
    x_ssem, x_rsem, zz_ssem, zz_rsem,
):
    blocks = seqs * reps
    my_seq = lax.axis_index("seq")
    my_rep = lax.axis_index("rep")
    me = my_seq * reps + my_rep
    mine = lax.axis_index("expert")
    row_size = CORES * DEPTH
    ys = experts // row_size
    my_y = mine // row_size
    my_z = lax.rem(mine, row_size) // CORES
    my_c = lax.rem(mine, CORES)

    def place_of(y, z, c):
        return {"expert": y * row_size + z * CORES + c}

    def hot_slot(c, y, z):
        return (c * ys + y) * DEPTH + z

    barrier = pltpu.get_barrier_semaphore()

    def greet(k, carry):
        pl.semaphore_signal(
            barrier, inc=1, device_id=group_device(lax.rem(me + k, blocks), reps),
            device_id_type=MESH,
        )
        return carry

    def greet_expert(k, carry):
        pl.semaphore_signal(
            barrier, inc=1, device_id={"expert": lax.rem(mine + k, experts)}, device_id_type=MESH
        )
        return carry

    lax.fori_loop(1, blocks, greet, 0)
    lax.fori_loop(1, experts, greet_expert, 0)
    load_up = pltpu.make_async_copy(up_hbm, up_ref, load_sem.at[0])
    load_down = pltpu.make_async_copy(down_hbm, down_ref, load_sem.at[1])
    load_up.start()
    load_down.start()
    for i, ref in enumerate((query_ref, key_ref, value_ref)):
        flipped = ref[...].astype(F32).T.astype(BF16)
        for h in range(blocks):
            heads[h, i * HD : (i + 1) * HD, :] = flipped[h * HD : (h + 1) * HD]
    starts = []
    for c in range(blocks * T // CHUNK):
        pos = lax.broadcasted_iota(jnp.int32, (1, CHUNK), 1) + c * CHUNK
        edge = jnp.int32(0)
        start = jnp.zeros((1, CHUNK), jnp.int32)
        for d in range(lengths_ref.shape[1] - 1):
            edge = edge + lengths_ref[0, d]
            start = jnp.where(pos >= edge, edge, start)
        starts.append(start)
    pl.semaphore_wait(barrier, blocks + experts - 2)

    def outgoing(k):
        to = lax.rem(me + k, blocks)
        return remote(
            heads.at[to], got.at[me], send_sem.at[to], recv_sem.at[me], group_device(to, reps)
        )

    def launch(k, carry):
        outgoing(k).start()
        return carry

    lax.fori_loop(1, blocks, launch, 0)
    got[me] = heads[me]

    def incoming(b):
        return remote(
            heads.at[b], got.at[b], send_sem.at[b], recv_sem.at[b], group_device(b, reps)
        )

    def returning(b):
        return remote(
            result.at[b], att.at[me], back_send_sem.at[b], back_recv_sem.at[me],
            group_device(b, reps),
        )

    per = CHUNK // T

    def give_back(c):
        for b in range(c * per, (c + 1) * per):

            @pl.when(me != b)
            def _():
                returning(b).start()

            @pl.when(me == b)
            def _():
                att[b] = result[b]

    chunks = blocks // per
    for c in range(chunks):
        for b in range(c * per, (c + 1) * per):

            @pl.when(me != b)
            def _():
                incoming(b).wait_recv()

            cols = pl.ds(b * T, T)
            q_all[:, cols] = got[b, 0:HD, :]
            v_all[:, cols] = got[b, 2 * HD : 3 * HD, :]
            k_all[cols, :] = got[b, HD : 2 * HD, :].astype(F32).T.astype(BF16)
        done = attend_chunk(c, starts[c], q_all, k_all, v_all)
        for j in range(per):
            result[c * per + j] = done[:, j * T : (j + 1) * T]
        if c:
            give_back(c - 1)

    chosen_row = row_ref[...]
    t_sub = lax.broadcasted_iota(jnp.int32, (T, T), 0)
    t_lane = lax.broadcasted_iota(jnp.int32, (T, T), 1)
    chosen_col = jnp.sum(jnp.where(t_sub == t_lane, chosen_row, 0), axis=1, keepdims=True)
    hits_t = chosen_row == lax.broadcasted_iota(jnp.int32, (experts, T), 0)
    hits = chosen_col == lax.broadcasted_iota(jnp.int32, (T, experts), 1)
    counts_t = jnp.sum(hits_t.astype(F32), axis=1, keepdims=True)
    counts = jnp.sum(hits.astype(F32), axis=0, keepdims=True)
    expert_ids = lax.broadcasted_iota(jnp.int32, (1, experts), 1)
    hot_id = jnp.max(jnp.where(counts > CAP, expert_ids, 0), axis=1, keepdims=True)
    hot_row = jnp.sum(jnp.where(hits_t, counts_t, 0.0), axis=0, keepdims=True) > CAP
    hot_col = jnp.sum(jnp.where(hits, counts, 0.0), axis=1, keepdims=True) > CAP
    ranks_t = jnp.dot(ones(hits_t), ones(t_sub < t_lane), preferred_element_type=F32)
    ranks = jnp.dot(ones(t_lane < t_sub), ones(hits), preferred_element_type=F32)
    rank_row = jnp.sum(jnp.where(hits_t, ranks_t, 0.0), axis=0, keepdims=True).astype(jnp.int32)
    rank_col = jnp.sum(jnp.where(hits, ranks, 0.0), axis=1, keepdims=True).astype(jnp.int32)
    nowhere = -1
    cold_slot_row = jnp.where(hot_row, nowhere, chosen_row * PAIR + rank_row)
    hot_slot_row = jnp.where(hot_row, rank_row, nowhere)
    cold_slot_col = jnp.where(hot_col, -PAIR, chosen_col * PAIR + rank_col)
    hot_slot_col = jnp.where(hot_col, rank_col, nowhere)
    slots = experts * PAIR
    slot_sub = lax.broadcasted_iota(jnp.int32, (slots, T), 0)
    place_rows = ones(slot_sub == cold_slot_row)
    place_grads = ones(
        slot_sub == jnp.where(hot_row, nowhere, chosen_row * PAIR + rank_row + CAP)
    )
    place_hot = ones(lax.broadcasted_iota(jnp.int32, (HOT, T), 0) == hot_slot_row)
    give_back(chunks - 1)

    def arrived(k, carry):
        b = lax.rem(me + k, blocks)
        remote(
            result.at[b], att.at[b], back_send_sem.at[b], back_recv_sem.at[b],
            group_device(b, reps),
        ).wait_recv()
        return carry

    lax.fori_loop(1, blocks, arrived, 0)
    attended = att[...].reshape(D, T).astype(F32).T.astype(BF16)
    mixed = (
        residual_ref[...].astype(F32)
        + jnp.dot(attended, proj_ref[...], preferred_element_type=F32)
    ).astype(BF16)
    mixed_f = mixed.astype(F32)
    inv_rms = lax.rsqrt(jnp.mean(mixed_f * mixed_f, axis=1, keepdims=True) + norm_eps)
    normed = (mixed_f * inv_rms).astype(BF16)
    last = (((1,), (1,)), ((), ()))
    first = (((0,), (0,)), ((), ()))
    logits = lax.dot_general(normed, router_ref[...], last, preferred_element_type=F32)
    gate = jax.nn.sigmoid(jnp.sum(jnp.where(hits, logits, 0.0), axis=1, keepdims=True))
    scaled = (gate * grad_ref[...].astype(F32)).astype(BF16)

    own_slot = hot_slot(my_c, my_y, my_z)
    hot_all[own_slot] = jnp.concatenate(
        [
            jnp.dot(place_hot, normed, preferred_element_type=F32),
            jnp.dot(place_hot, scaled, preferred_element_type=F32),
        ],
        axis=1,
    ).astype(BF16)
    placed = jnp.dot(place_rows, normed, preferred_element_type=F32) + jnp.dot(
        place_grads, scaled, preferred_element_type=F32
    )
    cold_send[...] = placed.astype(BF16).reshape(experts, PAIR, D)

    def z_copy(k):
        to = lax.rem(my_z + k, DEPTH)
        return remote(
            hot_all.at[own_slot], hot_all.at[own_slot], hz_ssem.at[k - 1], hz_rsem.at[my_z],
            place_of(my_y, to, my_c),
        )

    def z_arrival(z):
        slot = hot_slot(my_c, my_y, z)
        return remote(
            hot_all.at[slot], hot_all.at[slot], hz_ssem.at[0], hz_rsem.at[z],
            place_of(my_y, z, my_c),
        )

    def ring_copy(way, s, z):
        sign = 1 if way == 0 else -1
        block = lax.rem(my_y - sign * s + ys, ys)
        slot = hot_slot(my_c, block, z)
        return remote(
            hot_all.at[slot], hot_all.at[slot], ring_ssem.at[way, s, z], ring_rsem.at[way, s, z],
            place_of(lax.rem(my_y + sign + ys, ys), my_z, my_c),
        )

    def ring_block(way, s):
        sign = 1 if way == 0 else -1
        return lax.rem(my_y - sign * (s + 1) + ys, ys)

    def ring_arrival(way, s, z):
        sign = 1 if way == 0 else -1
        slot = hot_slot(my_c, ring_block(way, s), z)
        return remote(
            hot_all.at[slot], hot_all.at[slot], ring_ssem.at[way, s, z], ring_rsem.at[way, s, z],
            place_of(lax.rem(my_y - sign + ys, ys), my_z, my_c),
        )

    def to_sibling(y, z):
        slot = hot_slot(my_c, y, z)
        return remote(
            hot_all.at[slot], hot_all.at[slot], hc_ssem.at[y, z], hc_rsem.at[y, z],
            place_of(my_y, my_z, 1 - my_c),
        )

    def from_sibling(y, z):
        slot = hot_slot(1 - my_c, y, z)
        return remote(
            hot_all.at[slot], hot_all.at[slot], hc_ssem.at[y, z], hc_rsem.at[y, z],
            place_of(my_y, my_z, 1 - my_c),
        )

    for k in range(1, DEPTH):
        z_copy(k).start()

    def cold_copy(k):
        to = lax.rem(mine + k, experts)
        return remote(
            cold_send.at[to], cold_got.at[mine], cold_ssem.at[to], cold_rsem.at[mine],
            {"expert": to},
        )

    def start_cold(k, carry):
        cold_copy(k).start()
        return carry

    lax.fori_loop(1, experts, start_cold, 0)
    cold_got[mine] = cold_send[mine]
    ways = (ys // 2, ys - 1 - ys // 2)
    for t in range(DEPTH):
        z = lax.rem(my_z + t, DEPTH)
        if t:
            z_arrival(z).wait_recv()
        for way in range(2):
            ring_copy(way, 0, z).start()
        to_sibling(my_y, z).start()

    def ring_step(s):
        for t in range(DEPTH):
            z = lax.rem(my_z + t, DEPTH)
            for way in range(2):
                if s < ways[way]:
                    ring_arrival(way, s, z).wait_recv()
                    if s + 1 < ways[way]:
                        ring_copy(way, s + 1, z).start()
                    to_sibling(ring_block(way, s), z).start()

    for s in range(ways[0] - 1):
        ring_step(s)

    def cold_here(k, carry):
        b = lax.rem(mine + k, experts)
        remote(
            cold_send.at[b], cold_got.at[b], cold_ssem.at[b], cold_rsem.at[b], {"expert": b}
        ).wait_recv()
        return carry

    lax.fori_loop(1, experts, cold_here, 0)
    load_up.wait()
    load_down.wait()
    up = up_ref[...]
    down = down_ref[...]

    def expert_pass(tokens, grads_in):
        pre = jnp.dot(tokens, up, preferred_element_type=F32)
        sig = jax.nn.sigmoid(pre)
        activated = (pre * sig).astype(BF16)
        made = jnp.dot(activated, down, preferred_element_type=F32).astype(BF16)
        act_grad = lax.dot_general(grads_in, down, last, preferred_element_type=F32)
        pre_grad = (act_grad * sig * (1.0 + pre * (1.0 - sig))).astype(BF16)
        token_grad = lax.dot_general(pre_grad, up, last, preferred_element_type=F32).astype(BF16)
        return activated, pre_grad, made, token_grad

    cold_count = experts * CAP
    packed = cold_got[...].reshape(slots, D)
    cold_i = lax.broadcasted_iota(jnp.int32, (cold_count, slots), 0)
    pair_i = lax.broadcasted_iota(jnp.int32, (cold_count, slots), 1)
    spot = (cold_i // CAP) * PAIR + lax.rem(cold_i, CAP)
    take_rows = ones(pair_i == spot)
    take_grads = ones(pair_i == spot + CAP)
    cold_rows = jnp.dot(take_rows, packed, preferred_element_type=F32).astype(BF16)
    cold_grads = jnp.dot(take_grads, packed, preferred_element_type=F32).astype(BF16)
    cold_act, cold_pre, made, token_grad = expert_pass(cold_rows, cold_grads)
    repacked = lax.dot_general(take_rows, made, first, preferred_element_type=F32)
    repacked = repacked + lax.dot_general(
        take_grads, token_grad, first, preferred_element_type=F32
    )
    made_send[...] = repacked.astype(BF16).reshape(experts, PAIR, D)
    grad_up = lax.dot_general(cold_rows, cold_pre, first, preferred_element_type=F32)
    grad_down = lax.dot_general(cold_act, cold_grads, first, preferred_element_type=F32)

    def made_copy(k):
        to = lax.rem(mine + k, experts)
        return remote(
            made_send.at[to], made_got.at[mine], made_ssem.at[to], made_rsem.at[mine],
            {"expert": to},
        )

    def start_made(k, carry):
        made_copy(k).start()
        return carry

    lax.fori_loop(1, experts, start_made, 0)
    made_got[mine] = made_send[mine]
    ring_step(ways[0] - 1)
    for y in range(ys):
        for z in range(DEPTH):
            from_sibling(y, z).wait_recv()
    owner = (hot_id == mine).astype(F32)
    group = 16

    def hot_pass(i, carry):
        here = pl.ds(pl.multiple_of(i * group, group), group)
        flat = pl.ds(pl.multiple_of(i * group * HOT, group * HOT), group * HOT)
        both = hot_all[here].reshape(group * HOT, 2 * D)
        activated, pre_grad, hot_made, hot_grad = expert_pass(both[:, 0:D], both[:, D : 2 * D])
        hot_res[here, :, 0:D] = hot_made.reshape(group, HOT, D)
        hot_res[here, :, D : 2 * D] = hot_grad.reshape(group, HOT, D)
        act_ref[flat, :] = (activated.astype(F32) * owner).astype(BF16)
        pre_ref[flat, :] = (pre_grad.astype(F32) * owner).astype(BF16)
        return carry

    lax.fori_loop(0, experts // group, hot_pass, 0)
    hot_rows = hot_all[...].reshape(experts * HOT, 2 * D)
    grad_up = grad_up + lax.dot_general(
        hot_rows[:, 0:D], pre_ref[...], first, preferred_element_type=F32
    )

    half = experts // CORES
    core_copy = remote(
        hot_res.at[pl.ds((1 - my_c) * half, half)], core_got, core_ssem, core_rsem,
        place_of(my_y, my_z, 1 - my_c),
    )
    core_copy.start()
    grad_down = grad_down + lax.dot_general(
        act_ref[...], hot_rows[:, D : 2 * D], first, preferred_element_type=F32
    )
    share = D // blocks
    for m, grad in enumerate((grad_up, grad_down)):
        for j in range(blocks):
            grads[m, j % reps, j // reps] = grad[j * share : (j + 1) * share].astype(BF16)

    def along_x(m, k):
        to = lax.rem(my_rep + k, reps)
        return remote(
            grads.at[m, to], got_x.at[m, k - 1], x_ssem.at[m, k - 1], x_rsem.at[m, k - 1],
            {"rep": to},
        )

    def along_z(m, k):
        to = lax.rem(my_seq + k, seqs)
        return remote(
            part.at[m, to], got_zz.at[m, k - 1], zz_ssem.at[m, k - 1], zz_rsem.at[m, k - 1],
            {"seq": to},
        )

    hot_y = hot_id // row_size
    hot_z = lax.rem(hot_id, row_size) // CORES
    hot_c = lax.rem(hot_id, CORES)
    core_copy.wait_recv()
    for y in range(ys):
        for z in range(DEPTH):
            own = hot_res[hot_slot(my_c, y, z)].astype(F32)
            other = core_got[y * DEPTH + z].astype(F32)
            y_send[y, z] = jnp.where(hot_c == my_c, own, other).astype(BF16)
    for m in range(2):
        for k in range(1, reps):
            along_x(m, k).start()

    def y_copy(k):
        to = lax.rem(my_y + k, ys)
        return remote(
            y_send.at[to], y_got.at[my_y], y_ssem.at[to], y_rsem.at[my_y],
            place_of(to, my_z, my_c),
        )

    for k in range(1, ys):
        y_copy(k).start()
    y_got[my_y] = y_send[my_y]
    for m in range(2):
        for k in range(1, reps):
            along_x(m, k).wait_recv()
        for p in range(seqs):
            total = grads[m, my_rep, p].astype(F32)
            for k in range(1, reps):
                total = total + got_x[m, k - 1, p].astype(F32)
            part[m, p] = total.astype(BF16)
        for k in range(1, seqs):
            along_z(m, k).start()
    for k in range(1, ys):
        b = lax.rem(my_y + k, ys)
        remote(
            y_send.at[b], y_got.at[b], y_ssem.at[b], y_rsem.at[b], place_of(b, my_z, my_c)
        ).wait_recv()
    for z in range(DEPTH):
        kept = y_got[0, z].astype(F32)
        for y in range(1, ys):
            kept = jnp.where(hot_y == y, y_got[y, z].astype(F32), kept)
        z_send[z] = kept.astype(BF16)

    def made_here(k, carry):
        b = lax.rem(mine + k, experts)
        remote(
            made_send.at[b], made_got.at[b], made_ssem.at[b], made_rsem.at[b], {"expert": b}
        ).wait_recv()
        return carry

    lax.fori_loop(1, experts, made_here, 0)

    def down_copy(k):
        to = lax.rem(my_z + k, DEPTH)
        return remote(
            z_send.at[to], z_got.at[my_z], z_ssem.at[to], z_rsem.at[my_z],
            place_of(my_y, to, my_c),
        )

    for k in range(1, DEPTH):
        down_copy(k).start()
    z_got[my_z] = z_send[my_z]
    slot_lane = lax.broadcasted_iota(jnp.int32, (T, slots), 1)
    back = made_got[...].reshape(slots, D)
    result_f = jnp.dot(ones(slot_lane == cold_slot_col), back, preferred_element_type=F32)
    normed_grad = jnp.dot(
        ones(slot_lane == cold_slot_col + CAP), back, preferred_element_type=F32
    )
    router_cols = jnp.dot(ones(hits), router_ref[...], preferred_element_type=F32)
    for k in range(1, DEPTH):
        b = lax.rem(my_z + k, DEPTH)
        remote(
            z_send.at[b], z_got.at[b], z_ssem.at[b], z_rsem.at[b], place_of(my_y, b, my_c)
        ).wait_recv()
    kept = z_got[0].astype(F32)
    for z in range(1, DEPTH):
        kept = jnp.where(hot_z == z, z_got[z].astype(F32), kept)
    kept = kept.astype(BF16)
    pick_hot = ones(lax.broadcasted_iota(jnp.int32, (T, HOT), 1) == hot_slot_col)
    result_f = result_f + jnp.dot(pick_hot, kept[:, 0:D], preferred_element_type=F32)
    normed_grad = normed_grad + jnp.dot(
        pick_hot, kept[:, D : 2 * D], preferred_element_type=F32
    )
    grad_f = grad_ref[...].astype(F32)
    out_ref[...] = (mixed_f + gate * result_f).astype(BF16)
    gate_grad = jnp.sum(grad_f * result_f, axis=1, keepdims=True)
    logit_grad = gate_grad * gate * (1.0 - gate)
    total_grad = normed_grad + logit_grad * router_cols
    mean_term = jnp.mean(total_grad * mixed_f, axis=1, keepdims=True)
    input_grad = inv_rms * total_grad - mixed_f * inv_rms * inv_rms * inv_rms * mean_term
    grad_mixed_ref[...] = (grad_f + input_grad).astype(BF16)
    for m, ref in enumerate((share_in_ref, share_out_ref)):
        for k in range(1, seqs):
            along_z(m, k).wait_recv()
        total = part[m, my_seq].astype(F32)
        for k in range(1, seqs):
            total = total + got_zz[m, k - 1].astype(F32)
        ref[...] = total

    def sent_group(k, carry):
        outgoing(k).wait_send()
        returning(lax.rem(me + k, blocks)).wait_send()
        return carry

    def sent_experts(k, carry):
        cold_copy(k).wait_send()
        made_copy(k).wait_send()
        return carry

    lax.fori_loop(1, blocks, sent_group, 0)
    lax.fori_loop(1, experts, sent_experts, 0)
    for k in range(1, DEPTH):
        z_copy(k).wait_send()
        down_copy(k).wait_send()
    for way in range(2):
        for s in range(ways[way]):
            for z in range(DEPTH):
                ring_copy(way, s, z).wait_send()
    for y in range(ys):
        for z in range(DEPTH):
            to_sibling(y, z).wait_send()
    core_copy.wait_send()
    for k in range(1, ys):
        y_copy(k).wait_send()
    for m in range(2):
        for k in range(1, reps):
            along_x(m, k).wait_send()
        for k in range(1, seqs):
            along_z(m, k).wait_send()


def local(
    query_rows, key_rows, value_rows, doc_lengths, residual, out_proj, router, expert_choice,
    weight_in, weight_out, grad_out,
):
    seqs, reps = lax.axis_size("seq"), lax.axis_size("rep")
    blocks = seqs * reps
    experts = router.shape[1]
    share = D // blocks
    ys = experts // (CORES * DEPTH)
    dma = pltpu.SemaphoreType.DMA
    buffers = [
        (blocks, 3 * HD, T), (blocks, 3 * HD, T), (blocks, HD, T), (blocks, HD, T),
        (HD, blocks * T), (blocks * T, HD), (HD, blocks * T), (D, FF), (FF, D),
        (experts, PAIR, D), (experts, PAIR, D), (experts, PAIR, D), (experts, PAIR, D),
        (experts, HOT, 2 * D), (experts, HOT, 2 * D), (experts // CORES, HOT, 2 * D),
        (ys, DEPTH, HOT, 2 * D), (ys, DEPTH, HOT, 2 * D), (DEPTH, HOT, 2 * D),
        (DEPTH, HOT, 2 * D), (experts * HOT, FF), (experts * HOT, FF),
        (2, reps, seqs, share, FF), (2, reps - 1, seqs, share, FF), (2, seqs, share, FF),
        (2, seqs - 1, share, FF),
    ]
    semaphores = (
        [dma((2,))] + [dma((blocks,))] * 4 + [dma((experts,))] * 4
        + [dma((DEPTH - 1,)), dma((DEPTH,))]
        + [dma((2, ys // 2, DEPTH))] * 2 + [dma((ys, DEPTH))] * 2
        + [dma, dma] + [dma((ys,))] * 2 + [dma((DEPTH,))] * 2
        + [dma((2, reps - 1))] * 2 + [dma((2, seqs - 1))] * 2
    )
    anywhere = pl.BlockSpec(memory_space=pl.ANY)
    outs = pl.pallas_call(
        functools.partial(step_body, seqs, reps, experts),
        out_shape=(jax.ShapeDtypeStruct((T, D), BF16),) * 2
        + (jax.ShapeDtypeStruct((share, FF), F32),) * 2,
        in_specs=[pl.BlockSpec(memory_space=pltpu.SMEM)] + [VMEM] * 8 + [anywhere] * 2,
        out_specs=(VMEM,) * 4,
        scratch_shapes=[pltpu.VMEM(shape, BF16) for shape in buffers] + semaphores,
        compiler_params=pltpu.CompilerParams(collective_id=1, has_side_effects=True),
        name="step",
    )(
        doc_lengths, query_rows[0], key_rows[0], value_rows[0], residual[0], out_proj, router.T,
        expert_choice.reshape(1, T), grad_out[0], weight_in[0], weight_out[0],
    )
    return tuple(out[None] for out in outs)


def solution(mesh):
    rows = P("expert", ("seq", "rep"), None)
    weights = P("expert", None, None)
    in_specs = (
        rows, rows, rows, P("expert", None), rows, P(), P(), rows, weights, weights, rows,
    )
    return jax.shard_map(
        local, mesh=mesh, in_specs=in_specs, out_specs=(rows,) * 4, check_vma=False
    )
```

```python
import functools
import math

import jax
import jax.numpy as jnp
from jax import lax
from jax.experimental import pallas as pl
from jax.experimental.pallas import tpu as pltpu
from jax.sharding import PartitionSpec as P

D = 512
H = 16
HD = 32
FF = 512
T = 128
EXPERTS = 48
CAP = 4
HOT = 16
PAIR = 2 * CAP
CORES = 2
DEPTH = 3
WINDOW = 1024
CHUNK = 256
MESH = pl.DeviceIdType.MESH
norm_eps = 1e-06
masked_score = -1e30
F32 = jnp.float32
BF16 = jnp.bfloat16
VMEM = pl.BlockSpec(memory_space=pltpu.VMEM)


def group_device(rank, reps):
    return {"seq": rank // reps, "rep": lax.rem(rank, reps)}


def attend_chunk(c, start, q_all, k_all, v_all):
    scale = math.log2(math.e) / math.sqrt(HD)
    first_q = c * CHUNK
    first_k = max(0, first_q - WINDOW)
    span = first_q + CHUNK - first_k
    queries = pl.ds(first_q, CHUNK)
    scores = jnp.dot(
        k_all[pl.ds(first_k, span), :], q_all[:, queries], preferred_element_type=F32
    )
    key_pos = lax.broadcasted_iota(jnp.int32, (span, CHUNK), 0) + first_k
    query_pos = lax.broadcasted_iota(jnp.int32, (span, CHUNK), 1) + first_q
    visible = (key_pos >= start) & (key_pos <= query_pos)
    scores = jnp.where(visible, scores, masked_score)
    top = jnp.max(scores, axis=0, keepdims=True)
    weights = jnp.exp2((scores - top) * scale)
    totals = jnp.sum(weights, axis=0, keepdims=True)
    result = jnp.dot(
        v_all[:, pl.ds(first_k, span)], weights.astype(BF16), preferred_element_type=F32
    )
    return (result / totals).astype(BF16)


def remote(src, dst, send_sem, recv_sem, device):
    return pltpu.make_async_remote_copy(
        src_ref=src, dst_ref=dst, send_sem=send_sem, recv_sem=recv_sem, device_id=device,
        device_id_type=MESH,
    )


def ones(mask):
    return mask.astype(F32).astype(BF16)


def step_body(
    seqs, reps, experts,
    lengths_ref, query_ref, key_ref, value_ref, residual_ref, proj_ref, router_ref, row_ref,
    grad_ref, up_hbm, down_hbm,
    out_ref, grad_mixed_ref, share_in_ref, share_out_ref,
    heads, got, result, att, q_all, k_all, v_all, up_ref, down_ref,
    cold_send, cold_got, made_send, made_got,
    hot_all, hot_res, core_got, y_send, y_got, z_send, z_got,
    act_ref, pre_ref, grads, got_x, part, got_zz,
    load_sem, send_sem, recv_sem, back_send_sem, back_recv_sem,
    cold_ssem, cold_rsem, made_ssem, made_rsem,
    hz_ssem, hz_rsem, ring_ssem, ring_rsem, hc_ssem, hc_rsem,
    core_ssem, core_rsem, y_ssem, y_rsem, z_ssem, z_rsem,
    x_ssem, x_rsem, zz_ssem, zz_rsem,
):
    blocks = seqs * reps
    my_seq = lax.axis_index("seq")
    my_rep = lax.axis_index("rep")
    me = my_seq * reps + my_rep
    mine = lax.axis_index("expert")
    row_size = CORES * DEPTH
    ys = experts // row_size
    my_y = mine // row_size
    my_z = lax.rem(mine, row_size) // CORES
    my_c = lax.rem(mine, CORES)

    def place_of(y, z, c):
        return {"expert": y * row_size + z * CORES + c}

    def hot_slot(c, y, z):
        return (c * ys + y) * DEPTH + z

    barrier = pltpu.get_barrier_semaphore()

    def greet(k, carry):
        pl.semaphore_signal(
            barrier, inc=1, device_id=group_device(lax.rem(me + k, blocks), reps),
            device_id_type=MESH,
        )
        return carry

    def greet_expert(k, carry):
        pl.semaphore_signal(
            barrier, inc=1, device_id={"expert": lax.rem(mine + k, experts)}, device_id_type=MESH
        )
        return carry

    lax.fori_loop(1, blocks, greet, 0)
    lax.fori_loop(1, experts, greet_expert, 0)
    load_up = pltpu.make_async_copy(up_hbm, up_ref, load_sem.at[0])
    load_down = pltpu.make_async_copy(down_hbm, down_ref, load_sem.at[1])
    load_up.start()
    load_down.start()
    for i, ref in enumerate((query_ref, key_ref, value_ref)):
        flipped = ref[...].astype(F32).T.astype(BF16)
        for h in range(blocks):
            heads[h, i * HD : (i + 1) * HD, :] = flipped[h * HD : (h + 1) * HD]
    starts = []
    for c in range(blocks * T // CHUNK):
        pos = lax.broadcasted_iota(jnp.int32, (1, CHUNK), 1) + c * CHUNK
        edge = jnp.int32(0)
        start = jnp.zeros((1, CHUNK), jnp.int32)
        for d in range(lengths_ref.shape[1] - 1):
            edge = edge + lengths_ref[0, d]
            start = jnp.where(pos >= edge, edge, start)
        starts.append(start)
    pl.semaphore_wait(barrier, blocks + experts - 2)

    def outgoing(k):
        to = lax.rem(me + k, blocks)
        return remote(
            heads.at[to], got.at[me], send_sem.at[to], recv_sem.at[me], group_device(to, reps)
        )

    def launch(k, carry):
        outgoing(k).start()
        return carry

    lax.fori_loop(1, blocks, launch, 0)
    got[me] = heads[me]

    def incoming(b):
        return remote(
            heads.at[b], got.at[b], send_sem.at[b], recv_sem.at[b], group_device(b, reps)
        )

    def returning(b):
        return remote(
            result.at[b], att.at[me], back_send_sem.at[b], back_recv_sem.at[me],
            group_device(b, reps),
        )

    per = CHUNK // T

    def give_back(c):
        for b in range(c * per, (c + 1) * per):

            @pl.when(me != b)
            def _():
                returning(b).start()

            @pl.when(me == b)
            def _():
                att[b] = result[b]

    chunks = blocks // per
    for c in range(chunks):
        for b in range(c * per, (c + 1) * per):

            @pl.when(me != b)
            def _():
                incoming(b).wait_recv()

            cols = pl.ds(b * T, T)
            q_all[:, cols] = got[b, 0:HD, :]
            v_all[:, cols] = got[b, 2 * HD : 3 * HD, :]
            k_all[cols, :] = got[b, HD : 2 * HD, :].astype(F32).T.astype(BF16)
        done = attend_chunk(c, starts[c], q_all, k_all, v_all)
        for j in range(per):
            result[c * per + j] = done[:, j * T : (j + 1) * T]
        if c:
            give_back(c - 1)

    chosen_row = row_ref[...]
    t_sub = lax.broadcasted_iota(jnp.int32, (T, T), 0)
    t_lane = lax.broadcasted_iota(jnp.int32, (T, T), 1)
    chosen_col = jnp.sum(jnp.where(t_sub == t_lane, chosen_row, 0), axis=1, keepdims=True)
    hits_t = chosen_row == lax.broadcasted_iota(jnp.int32, (experts, T), 0)
    hits = chosen_col == lax.broadcasted_iota(jnp.int32, (T, experts), 1)
    counts_t = jnp.sum(hits_t.astype(F32), axis=1, keepdims=True)
    counts = jnp.sum(hits.astype(F32), axis=0, keepdims=True)
    expert_ids = lax.broadcasted_iota(jnp.int32, (1, experts), 1)
    hot_id = jnp.max(jnp.where(counts > CAP, expert_ids, 0), axis=1, keepdims=True)
    hot_row = jnp.sum(jnp.where(hits_t, counts_t, 0.0), axis=0, keepdims=True) > CAP
    hot_col = jnp.sum(jnp.where(hits, counts, 0.0), axis=1, keepdims=True) > CAP
    ranks_t = jnp.dot(ones(hits_t), ones(t_sub < t_lane), preferred_element_type=F32)
    ranks = jnp.dot(ones(t_lane < t_sub), ones(hits), preferred_element_type=F32)
    rank_row = jnp.sum(jnp.where(hits_t, ranks_t, 0.0), axis=0, keepdims=True).astype(jnp.int32)
    rank_col = jnp.sum(jnp.where(hits, ranks, 0.0), axis=1, keepdims=True).astype(jnp.int32)
    nowhere = -1
    cold_slot_row = jnp.where(hot_row, nowhere, chosen_row * PAIR + rank_row)
    hot_slot_row = jnp.where(hot_row, rank_row, nowhere)
    cold_slot_col = jnp.where(hot_col, -PAIR, chosen_col * PAIR + rank_col)
    hot_slot_col = jnp.where(hot_col, rank_col, nowhere)
    slots = experts * PAIR
    slot_sub = lax.broadcasted_iota(jnp.int32, (slots, T), 0)
    place_rows = ones(slot_sub == cold_slot_row)
    place_grads = ones(
        slot_sub == jnp.where(hot_row, nowhere, chosen_row * PAIR + rank_row + CAP)
    )
    place_hot = ones(lax.broadcasted_iota(jnp.int32, (HOT, T), 0) == hot_slot_row)
    give_back(chunks - 1)

    def arrived(k, carry):
        b = lax.rem(me + k, blocks)
        remote(
            result.at[b], att.at[b], back_send_sem.at[b], back_recv_sem.at[b],
            group_device(b, reps),
        ).wait_recv()
        return carry

    lax.fori_loop(1, blocks, arrived, 0)
    attended = att[...].reshape(D, T).astype(F32).T.astype(BF16)
    mixed = (
        residual_ref[...].astype(F32)
        + jnp.dot(attended, proj_ref[...], preferred_element_type=F32)
    ).astype(BF16)
    mixed_f = mixed.astype(F32)
    inv_rms = lax.rsqrt(jnp.mean(mixed_f * mixed_f, axis=1, keepdims=True) + norm_eps)
    normed = (mixed_f * inv_rms).astype(BF16)
    last = (((1,), (1,)), ((), ()))
    first = (((0,), (0,)), ((), ()))
    logits = lax.dot_general(normed, router_ref[...], last, preferred_element_type=F32)
    gate = jax.nn.sigmoid(jnp.sum(jnp.where(hits, logits, 0.0), axis=1, keepdims=True))
    scaled = (gate * grad_ref[...].astype(F32)).astype(BF16)

    own_slot = hot_slot(my_c, my_y, my_z)
    hot_all[own_slot] = jnp.concatenate(
        [
            jnp.dot(place_hot, normed, preferred_element_type=F32),
            jnp.dot(place_hot, scaled, preferred_element_type=F32),
        ],
        axis=1,
    ).astype(BF16)
    placed = jnp.dot(place_rows, normed, preferred_element_type=F32) + jnp.dot(
        place_grads, scaled, preferred_element_type=F32
    )
    cold_send[...] = placed.astype(BF16).reshape(experts, PAIR, D)

    def z_copy(k):
        to = lax.rem(my_z + k, DEPTH)
        return remote(
            hot_all.at[own_slot], hot_all.at[own_slot], hz_ssem.at[k - 1], hz_rsem.at[my_z],
            place_of(my_y, to, my_c),
        )

    def z_arrival(z):
        slot = hot_slot(my_c, my_y, z)
        return remote(
            hot_all.at[slot], hot_all.at[slot], hz_ssem.at[0], hz_rsem.at[z],
            place_of(my_y, z, my_c),
        )

    def ring_copy(way, s, z):
        sign = 1 if way == 0 else -1
        block = lax.rem(my_y - sign * s + ys, ys)
        slot = hot_slot(my_c, block, z)
        return remote(
            hot_all.at[slot], hot_all.at[slot], ring_ssem.at[way, s, z], ring_rsem.at[way, s, z],
            place_of(lax.rem(my_y + sign + ys, ys), my_z, my_c),
        )

    def ring_block(way, s):
        sign = 1 if way == 0 else -1
        return lax.rem(my_y - sign * (s + 1) + ys, ys)

    def ring_arrival(way, s, z):
        sign = 1 if way == 0 else -1
        slot = hot_slot(my_c, ring_block(way, s), z)
        return remote(
            hot_all.at[slot], hot_all.at[slot], ring_ssem.at[way, s, z], ring_rsem.at[way, s, z],
            place_of(lax.rem(my_y - sign + ys, ys), my_z, my_c),
        )

    def to_sibling(y, z):
        slot = hot_slot(my_c, y, z)
        return remote(
            hot_all.at[slot], hot_all.at[slot], hc_ssem.at[y, z], hc_rsem.at[y, z],
            place_of(my_y, my_z, 1 - my_c),
        )

    def from_sibling(y, z):
        slot = hot_slot(1 - my_c, y, z)
        return remote(
            hot_all.at[slot], hot_all.at[slot], hc_ssem.at[y, z], hc_rsem.at[y, z],
            place_of(my_y, my_z, 1 - my_c),
        )

    def ring_start(t):
        z = lax.rem(my_z + t, DEPTH)
        if t:
            z_arrival(z).wait_recv()
        for way in range(2):
            ring_copy(way, 0, z).start()
        to_sibling(my_y, z).start()

    for k in range(1, DEPTH):
        z_copy(k).start()
    ring_start(0)

    def cold_copy(k):
        to = lax.rem(mine + k, experts)
        return remote(
            cold_send.at[to], cold_got.at[mine], cold_ssem.at[to], cold_rsem.at[mine],
            {"expert": to},
        )

    def start_cold(k, carry):
        cold_copy(k).start()
        return carry

    lax.fori_loop(1, experts, start_cold, 0)
    cold_got[mine] = cold_send[mine]
    ways = (ys // 2, ys - 1 - ys // 2)
    for t in range(1, DEPTH):
        ring_start(t)

    def ring_step(s):
        for t in range(DEPTH):
            z = lax.rem(my_z + t, DEPTH)
            for way in range(2):
                if s < ways[way]:
                    ring_arrival(way, s, z).wait_recv()
                    if s + 1 < ways[way]:
                        ring_copy(way, s + 1, z).start()
                    to_sibling(ring_block(way, s), z).start()

    def cold_here(k, carry):
        b = lax.rem(mine + k, experts)
        remote(
            cold_send.at[b], cold_got.at[b], cold_ssem.at[b], cold_rsem.at[b], {"expert": b}
        ).wait_recv()
        return carry

    load_up.wait()
    load_down.wait()
    up = up_ref[...]
    down = down_ref[...]

    def expert_pass(tokens, grads_in):
        pre = jnp.dot(tokens, up, preferred_element_type=F32)
        sig = jax.nn.sigmoid(pre)
        activated = (pre * sig).astype(BF16)
        made = jnp.dot(activated, down, preferred_element_type=F32).astype(BF16)
        act_grad = lax.dot_general(grads_in, down, last, preferred_element_type=F32)
        pre_grad = (act_grad * sig * (1.0 + pre * (1.0 - sig))).astype(BF16)
        token_grad = lax.dot_general(pre_grad, up, last, preferred_element_type=F32).astype(BF16)
        return activated, pre_grad, made, token_grad

    owner = (hot_id == mine).astype(F32)

    def core_copy(b):
        return remote(
            hot_res.at[pl.ds(hot_slot(1 - my_c, b, 0), DEPTH)],
            core_got.at[pl.ds(b * DEPTH, DEPTH)], core_ssem.at[b], core_rsem.at[b],
            place_of(my_y, my_z, 1 - my_c),
        )

    def pair_of(p):
        if p + 1 < ways[0]:
            return [lax.rem(my_y - p - 1 + ys, ys), lax.rem(my_y + p + 1, ys)]
        return [lax.rem(my_y + ways[0], ys), my_y]

    def hot_pass(p):
        where = []
        for b in pair_of(p):
            for z in range(DEPTH):
                from_sibling(b, z).wait_recv()
            where += [hot_slot(c, b, 0) for c in range(CORES)]
        size = DEPTH * HOT
        both = jnp.concatenate(
            [hot_all[pl.ds(slot, DEPTH)].reshape(size, 2 * D) for slot in where], axis=0
        )
        activated, pre_grad, hot_made, hot_grad = expert_pass(both[:, 0:D], both[:, D : 2 * D])
        kept_act = (activated.astype(F32) * owner).astype(BF16)
        kept_pre = (pre_grad.astype(F32) * owner).astype(BF16)
        for i, slot in enumerate(where):
            rows = slice(i * size, (i + 1) * size)
            here = pl.ds(slot, DEPTH)
            hot_res[here, :, 0:D] = hot_made[rows].reshape(DEPTH, HOT, D)
            hot_res[here, :, D : 2 * D] = hot_grad[rows].reshape(DEPTH, HOT, D)
            act_ref[here] = kept_act[rows].reshape(DEPTH, HOT, FF)
            pre_ref[here] = kept_pre[rows].reshape(DEPTH, HOT, FF)

    def core_start(p):
        for b in pair_of(p):
            core_copy(b).start()

    hot_y = hot_id // row_size
    hot_z = lax.rem(hot_id, row_size) // CORES
    hot_c = lax.rem(hot_id, CORES)

    def y_copy(b):
        return remote(
            y_send.at[b], y_got.at[my_y], y_ssem.at[b], y_rsem.at[my_y],
            place_of(b, my_z, my_c),
        )

    def y_fill(p):
        for b in pair_of(p):
            remote(
                hot_res.at[pl.ds(hot_slot(1 - my_c, b, 0), DEPTH)],
                core_got.at[pl.ds(b * DEPTH, DEPTH)], core_ssem.at[b], core_rsem.at[b],
                place_of(my_y, my_z, 1 - my_c),
            ).wait_recv()
            own = hot_res[pl.ds(hot_slot(my_c, b, 0), DEPTH)].astype(F32)
            other = core_got[pl.ds(b * DEPTH, DEPTH)].astype(F32)
            y_send[b] = jnp.where(hot_c == my_c, own, other).astype(BF16)

    def y_start(p):
        here = pair_of(p)
        if p + 1 == ways[0]:
            here = here[:1]
        for b in here:
            y_copy(b).start()

    ring_step(0)
    ring_step(1)
    hot_pass(0)
    lax.fori_loop(1, experts, cold_here, 0)
    core_start(0)
    cold_count = experts * CAP
    packed = cold_got[...].reshape(slots, D)
    cold_i = lax.broadcasted_iota(jnp.int32, (cold_count, slots), 0)
    pair_i = lax.broadcasted_iota(jnp.int32, (cold_count, slots), 1)
    spot = (cold_i // CAP) * PAIR + lax.rem(cold_i, CAP)
    take_rows = ones(pair_i == spot)
    take_grads = ones(pair_i == spot + CAP)
    cold_rows = jnp.dot(take_rows, packed, preferred_element_type=F32).astype(BF16)
    cold_grads = jnp.dot(take_grads, packed, preferred_element_type=F32).astype(BF16)
    cold_act, cold_pre, made, token_grad = expert_pass(cold_rows, cold_grads)
    repacked = lax.dot_general(take_rows, made, first, preferred_element_type=F32)
    repacked = repacked + lax.dot_general(
        take_grads, token_grad, first, preferred_element_type=F32
    )
    made_send[...] = repacked.astype(BF16).reshape(experts, PAIR, D)
    grad_up = lax.dot_general(cold_rows, cold_pre, first, preferred_element_type=F32)
    grad_down = lax.dot_general(cold_act, cold_grads, first, preferred_element_type=F32)

    def made_copy(k):
        to = lax.rem(mine + k, experts)
        return remote(
            made_send.at[to], made_got.at[mine], made_ssem.at[to], made_rsem.at[mine],
            {"expert": to},
        )

    def start_made(k, carry):
        made_copy(k).start()
        return carry

    lax.fori_loop(1, experts, start_made, 0)
    made_got[mine] = made_send[mine]
    for p in range(1, ways[0] - 1):
        ring_step(p + 1)
        hot_pass(p)
        y_fill(p - 1)
        core_start(p)
        y_start(p - 1)
    hot_pass(ways[0] - 1)
    y_fill(ways[0] - 2)
    core_start(ways[0] - 1)
    y_start(ways[0] - 2)
    share = D // blocks

    def store_grad(m, grad):
        for j in range(blocks):
            grads[m, j % reps, j // reps] = grad[j * share : (j + 1) * share].astype(BF16)

    hot_count = experts * HOT
    hot_rows = hot_all[...].reshape(hot_count, 2 * D)
    grad_up = grad_up + lax.dot_general(
        hot_rows[:, 0:D], pre_ref[...].reshape(hot_count, FF), first, preferred_element_type=F32
    )
    store_grad(0, grad_up)
    y_fill(ways[0] - 1)

    def along_x(m, k):
        to = lax.rem(my_rep + k, reps)
        return remote(
            grads.at[m, to], got_x.at[m, k - 1], x_ssem.at[m, k - 1], x_rsem.at[m, k - 1],
            {"rep": to},
        )

    def along_z(m, k):
        to = lax.rem(my_seq + k, seqs)
        return remote(
            part.at[m, to], got_zz.at[m, k - 1], zz_ssem.at[m, k - 1], zz_rsem.at[m, k - 1],
            {"seq": to},
        )

    for k in range(1, reps):
        along_x(0, k).start()
    y_start(ways[0] - 1)
    grad_down = grad_down + lax.dot_general(
        act_ref[...].reshape(hot_count, FF), hot_rows[:, D : 2 * D], first,
        preferred_element_type=F32,
    )
    store_grad(1, grad_down)
    y_got[my_y] = y_send[my_y]
    for k in range(1, reps):
        along_x(1, k).start()
    for m in range(2):
        for k in range(1, reps):
            along_x(m, k).wait_recv()
        for p in range(seqs):
            total = grads[m, my_rep, p].astype(F32)
            for k in range(1, reps):
                total = total + got_x[m, k - 1, p].astype(F32)
            part[m, p] = total.astype(BF16)
        for k in range(1, seqs):
            along_z(m, k).start()
    for k in range(1, ys):
        b = lax.rem(my_y + k, ys)
        remote(
            y_send.at[b], y_got.at[b], y_ssem.at[b], y_rsem.at[b], place_of(b, my_z, my_c)
        ).wait_recv()
    for z in range(DEPTH):
        kept = y_got[0, z].astype(F32)
        for y in range(1, ys):
            kept = jnp.where(hot_y == y, y_got[y, z].astype(F32), kept)
        z_send[z] = kept.astype(BF16)

    def made_here(k, carry):
        b = lax.rem(mine + k, experts)
        remote(
            made_send.at[b], made_got.at[b], made_ssem.at[b], made_rsem.at[b], {"expert": b}
        ).wait_recv()
        return carry

    lax.fori_loop(1, experts, made_here, 0)

    def down_copy(k):
        to = lax.rem(my_z + k, DEPTH)
        return remote(
            z_send.at[to], z_got.at[my_z], z_ssem.at[to], z_rsem.at[my_z],
            place_of(my_y, to, my_c),
        )

    for k in range(1, DEPTH):
        down_copy(k).start()
    z_got[my_z] = z_send[my_z]
    slot_lane = lax.broadcasted_iota(jnp.int32, (T, slots), 1)
    back = made_got[...].reshape(slots, D)
    result_f = jnp.dot(ones(slot_lane == cold_slot_col), back, preferred_element_type=F32)
    normed_grad = jnp.dot(
        ones(slot_lane == cold_slot_col + CAP), back, preferred_element_type=F32
    )
    router_cols = jnp.dot(ones(hits), router_ref[...], preferred_element_type=F32)
    for k in range(1, DEPTH):
        b = lax.rem(my_z + k, DEPTH)
        remote(
            z_send.at[b], z_got.at[b], z_ssem.at[b], z_rsem.at[b], place_of(my_y, b, my_c)
        ).wait_recv()
    kept = z_got[0].astype(F32)
    for z in range(1, DEPTH):
        kept = jnp.where(hot_z == z, z_got[z].astype(F32), kept)
    kept = kept.astype(BF16)
    pick_hot = ones(lax.broadcasted_iota(jnp.int32, (T, HOT), 1) == hot_slot_col)
    result_f = result_f + jnp.dot(pick_hot, kept[:, 0:D], preferred_element_type=F32)
    normed_grad = normed_grad + jnp.dot(
        pick_hot, kept[:, D : 2 * D], preferred_element_type=F32
    )
    grad_f = grad_ref[...].astype(F32)
    out_ref[...] = (mixed_f + gate * result_f).astype(BF16)
    gate_grad = jnp.sum(grad_f * result_f, axis=1, keepdims=True)
    logit_grad = gate_grad * gate * (1.0 - gate)
    total_grad = normed_grad + logit_grad * router_cols
    mean_term = jnp.mean(total_grad * mixed_f, axis=1, keepdims=True)
    input_grad = inv_rms * total_grad - mixed_f * inv_rms * inv_rms * inv_rms * mean_term
    grad_mixed_ref[...] = (grad_f + input_grad).astype(BF16)
    for m, ref in enumerate((share_in_ref, share_out_ref)):
        for k in range(1, seqs):
            along_z(m, k).wait_recv()
        total = part[m, my_seq].astype(F32)
        for k in range(1, seqs):
            total = total + got_zz[m, k - 1].astype(F32)
        ref[...] = total

    def sent_group(k, carry):
        outgoing(k).wait_send()
        returning(lax.rem(me + k, blocks)).wait_send()
        return carry

    def sent_experts(k, carry):
        cold_copy(k).wait_send()
        made_copy(k).wait_send()
        return carry

    lax.fori_loop(1, blocks, sent_group, 0)
    lax.fori_loop(1, experts, sent_experts, 0)
    for k in range(1, DEPTH):
        z_copy(k).wait_send()
        down_copy(k).wait_send()
    for way in range(2):
        for s in range(ways[way]):
            for z in range(DEPTH):
                ring_copy(way, s, z).wait_send()
    for y in range(ys):
        for z in range(DEPTH):
            to_sibling(y, z).wait_send()
    for b in range(ys):
        core_copy(b).wait_send()
    for k in range(1, ys):
        y_copy(lax.rem(my_y + k, ys)).wait_send()
    for m in range(2):
        for k in range(1, reps):
            along_x(m, k).wait_send()
        for k in range(1, seqs):
            along_z(m, k).wait_send()


def local(
    query_rows, key_rows, value_rows, doc_lengths, residual, out_proj, router, expert_choice,
    weight_in, weight_out, grad_out,
):
    seqs, reps = lax.axis_size("seq"), lax.axis_size("rep")
    blocks = seqs * reps
    experts = router.shape[1]
    share = D // blocks
    ys = experts // (CORES * DEPTH)
    dma = pltpu.SemaphoreType.DMA
    buffers = [
        (blocks, 3 * HD, T), (blocks, 3 * HD, T), (blocks, HD, T), (blocks, HD, T),
        (HD, blocks * T), (blocks * T, HD), (HD, blocks * T), (D, FF), (FF, D),
        (experts, PAIR, D), (experts, PAIR, D), (experts, PAIR, D), (experts, PAIR, D),
        (experts, HOT, 2 * D), (experts, HOT, 2 * D), (experts // CORES, HOT, 2 * D),
        (ys, DEPTH, HOT, 2 * D), (ys, DEPTH, HOT, 2 * D), (DEPTH, HOT, 2 * D),
        (DEPTH, HOT, 2 * D), (experts, HOT, FF), (experts, HOT, FF),
        (2, reps, seqs, share, FF), (2, reps - 1, seqs, share, FF), (2, seqs, share, FF),
        (2, seqs - 1, share, FF),
    ]
    semaphores = (
        [dma((2,))] + [dma((blocks,))] * 4 + [dma((experts,))] * 4
        + [dma((DEPTH - 1,)), dma((DEPTH,))]
        + [dma((2, ys // 2, DEPTH))] * 2 + [dma((ys, DEPTH))] * 2
        + [dma((ys,))] * 4 + [dma((DEPTH,))] * 2
        + [dma((2, reps - 1))] * 2 + [dma((2, seqs - 1))] * 2
    )
    anywhere = pl.BlockSpec(memory_space=pl.ANY)
    outs = pl.pallas_call(
        functools.partial(step_body, seqs, reps, experts),
        out_shape=(jax.ShapeDtypeStruct((T, D), BF16),) * 2
        + (jax.ShapeDtypeStruct((share, FF), F32),) * 2,
        in_specs=[pl.BlockSpec(memory_space=pltpu.SMEM)] + [VMEM] * 8 + [anywhere] * 2,
        out_specs=(VMEM,) * 4,
        scratch_shapes=[pltpu.VMEM(shape, BF16) for shape in buffers] + semaphores,
        compiler_params=pltpu.CompilerParams(collective_id=1, has_side_effects=True),
        name="step",
    )(
        doc_lengths, query_rows[0], key_rows[0], value_rows[0], residual[0], out_proj, router.T,
        expert_choice.reshape(1, T), grad_out[0], weight_in[0], weight_out[0],
    )
    return tuple(out[None] for out in outs)


def solution(mesh):
    rows = P("expert", ("seq", "rep"), None)
    weights = P("expert", None, None)
    in_specs = (
        rows, rows, rows, P("expert", None), rows, P(), P(), rows, weights, weights, rows,
    )
    return jax.shard_map(
        local, mesh=mesh, in_specs=in_specs, out_specs=(rows,) * 4, check_vma=False
    )
```

```python
import functools
import math

import jax
import jax.numpy as jnp
from jax import lax
from jax.experimental import pallas as pl
from jax.experimental.pallas import tpu as pltpu
from jax.sharding import PartitionSpec as P

D = 512
H = 16
HD = 32
FF = 512
T = 128
EXPERTS = 48
CAP = 4
HOT = 16
PAIR = 2 * CAP
CORES = 2
DEPTH = 3
WINDOW = 1024
CHUNK = 256
MESH = pl.DeviceIdType.MESH
norm_eps = 1e-06
masked_score = -1e30
F32 = jnp.float32
BF16 = jnp.bfloat16
VMEM = pl.BlockSpec(memory_space=pltpu.VMEM)


def group_device(rank, reps):
    return {"seq": rank // reps, "rep": lax.rem(rank, reps)}


def attend_chunk(c, start, q_all, k_all, v_all):
    scale = math.log2(math.e) / math.sqrt(HD)
    first_q = c * CHUNK
    first_k = max(0, first_q - WINDOW)
    span = first_q + CHUNK - first_k
    queries = pl.ds(first_q, CHUNK)
    scores = jnp.dot(
        k_all[pl.ds(first_k, span), :], q_all[:, queries], preferred_element_type=F32
    )
    key_pos = lax.broadcasted_iota(jnp.int32, (span, CHUNK), 0) + first_k
    query_pos = lax.broadcasted_iota(jnp.int32, (span, CHUNK), 1) + first_q
    visible = (key_pos >= start) & (key_pos <= query_pos)
    scores = jnp.where(visible, scores, masked_score)
    top = jnp.max(scores, axis=0, keepdims=True)
    weights = jnp.exp2((scores - top) * scale)
    totals = jnp.sum(weights, axis=0, keepdims=True)
    result = jnp.dot(
        v_all[:, pl.ds(first_k, span)], weights.astype(BF16), preferred_element_type=F32
    )
    return (result / totals).astype(BF16)


def remote(src, dst, send_sem, recv_sem, device):
    return pltpu.make_async_remote_copy(
        src_ref=src, dst_ref=dst, send_sem=send_sem, recv_sem=recv_sem, device_id=device,
        device_id_type=MESH,
    )


def ones(mask):
    return mask.astype(F32).astype(BF16)


def step_body(
    seqs, reps, experts,
    lengths_ref, query_ref, key_ref, value_ref, residual_ref, proj_ref, router_ref, row_ref,
    grad_ref, up_hbm, down_hbm,
    out_ref, grad_mixed_ref, share_in_ref, share_out_ref,
    heads, got, result, att, q_all, k_all, v_all, up_ref, down_ref,
    cold_send, cold_got, made_send, made_got,
    hot_all, hot_res, core_got, y_send, y_got, z_send, z_got,
    act_ref, pre_ref, grads, got_x, part, got_zz,
    load_sem, send_sem, recv_sem, back_send_sem, back_recv_sem,
    cold_ssem, cold_rsem, made_ssem, made_rsem,
    hz_ssem, hz_rsem, ring_ssem, ring_rsem, hc_ssem, hc_rsem,
    core_ssem, core_rsem, y_ssem, y_rsem, z_ssem, z_rsem,
    x_ssem, x_rsem, zz_ssem, zz_rsem,
):
    blocks = seqs * reps
    my_seq = lax.axis_index("seq")
    my_rep = lax.axis_index("rep")
    me = my_seq * reps + my_rep
    mine = lax.axis_index("expert")
    row_size = CORES * DEPTH
    ys = experts // row_size
    my_y = mine // row_size
    my_z = lax.rem(mine, row_size) // CORES
    my_c = lax.rem(mine, CORES)

    def place_of(y, z, c):
        return {"expert": y * row_size + z * CORES + c}

    def hot_slot(c, y, z):
        return (c * ys + y) * DEPTH + z

    barrier = pltpu.get_barrier_semaphore()

    def greet(k, carry):
        pl.semaphore_signal(
            barrier, inc=1, device_id=group_device(lax.rem(me + k, blocks), reps),
            device_id_type=MESH,
        )
        return carry

    def greet_expert(k, carry):
        pl.semaphore_signal(
            barrier, inc=1, device_id={"expert": lax.rem(mine + k, experts)}, device_id_type=MESH
        )
        return carry

    lax.fori_loop(1, blocks, greet, 0)
    lax.fori_loop(1, experts, greet_expert, 0)
    load_up = pltpu.make_async_copy(up_hbm, up_ref, load_sem.at[0])
    load_down = pltpu.make_async_copy(down_hbm, down_ref, load_sem.at[1])
    load_up.start()
    load_down.start()
    for i, ref in enumerate((query_ref, key_ref, value_ref)):
        flipped = ref[...].astype(F32).T.astype(BF16)
        for h in range(blocks):
            heads[h, i * HD : (i + 1) * HD, :] = flipped[h * HD : (h + 1) * HD]
    starts = []
    for c in range(blocks * T // CHUNK):
        pos = lax.broadcasted_iota(jnp.int32, (1, CHUNK), 1) + c * CHUNK
        edge = jnp.int32(0)
        start = jnp.zeros((1, CHUNK), jnp.int32)
        for d in range(lengths_ref.shape[1] - 1):
            edge = edge + lengths_ref[0, d]
            start = jnp.where(pos >= edge, edge, start)
        starts.append(start)
    pl.semaphore_wait(barrier, blocks + experts - 2)

    def outgoing(k):
        to = lax.rem(me + k, blocks)
        return remote(
            heads.at[to], got.at[me], send_sem.at[to], recv_sem.at[me], group_device(to, reps)
        )

    def launch(k, carry):
        outgoing(k).start()
        return carry

    lax.fori_loop(1, blocks, launch, 0)
    got[me] = heads[me]

    def incoming(b):
        return remote(
            heads.at[b], got.at[b], send_sem.at[b], recv_sem.at[b], group_device(b, reps)
        )

    def returning(b):
        return remote(
            result.at[b], att.at[me], back_send_sem.at[b], back_recv_sem.at[me],
            group_device(b, reps),
        )

    per = CHUNK // T

    def give_back(c):
        for b in range(c * per, (c + 1) * per):

            @pl.when(me != b)
            def _():
                returning(b).start()

            @pl.when(me == b)
            def _():
                att[b] = result[b]

    chunks = blocks // per
    for c in range(chunks):
        for b in range(c * per, (c + 1) * per):

            @pl.when(me != b)
            def _():
                incoming(b).wait_recv()

            cols = pl.ds(b * T, T)
            q_all[:, cols] = got[b, 0:HD, :]
            v_all[:, cols] = got[b, 2 * HD : 3 * HD, :]
            k_all[cols, :] = got[b, HD : 2 * HD, :].astype(F32).T.astype(BF16)
        done = attend_chunk(c, starts[c], q_all, k_all, v_all)
        for j in range(per):
            result[c * per + j] = done[:, j * T : (j + 1) * T]
        if c:
            give_back(c - 1)

    chosen_row = row_ref[...]
    t_sub = lax.broadcasted_iota(jnp.int32, (T, T), 0)
    t_lane = lax.broadcasted_iota(jnp.int32, (T, T), 1)
    chosen_col = jnp.sum(jnp.where(t_sub == t_lane, chosen_row, 0), axis=1, keepdims=True)
    hits_t = chosen_row == lax.broadcasted_iota(jnp.int32, (experts, T), 0)
    hits = chosen_col == lax.broadcasted_iota(jnp.int32, (T, experts), 1)
    counts_t = jnp.sum(hits_t.astype(F32), axis=1, keepdims=True)
    counts = jnp.sum(hits.astype(F32), axis=0, keepdims=True)
    expert_ids = lax.broadcasted_iota(jnp.int32, (1, experts), 1)
    hot_id = jnp.max(jnp.where(counts > CAP, expert_ids, 0), axis=1, keepdims=True)
    hot_row = jnp.sum(jnp.where(hits_t, counts_t, 0.0), axis=0, keepdims=True) > CAP
    hot_col = jnp.sum(jnp.where(hits, counts, 0.0), axis=1, keepdims=True) > CAP
    ranks_t = jnp.dot(ones(hits_t), ones(t_sub < t_lane), preferred_element_type=F32)
    ranks = jnp.dot(ones(t_lane < t_sub), ones(hits), preferred_element_type=F32)
    rank_row = jnp.sum(jnp.where(hits_t, ranks_t, 0.0), axis=0, keepdims=True).astype(jnp.int32)
    rank_col = jnp.sum(jnp.where(hits, ranks, 0.0), axis=1, keepdims=True).astype(jnp.int32)
    nowhere = -1
    cold_slot_row = jnp.where(hot_row, nowhere, chosen_row * PAIR + rank_row)
    hot_slot_row = jnp.where(hot_row, rank_row, nowhere)
    cold_slot_col = jnp.where(hot_col, -PAIR, chosen_col * PAIR + rank_col)
    hot_slot_col = jnp.where(hot_col, rank_col, nowhere)
    slots = experts * PAIR
    slot_sub = lax.broadcasted_iota(jnp.int32, (slots, T), 0)
    place_rows = ones(slot_sub == cold_slot_row)
    place_grads = ones(
        slot_sub == jnp.where(hot_row, nowhere, chosen_row * PAIR + rank_row + CAP)
    )
    place_hot = ones(lax.broadcasted_iota(jnp.int32, (HOT, T), 0) == hot_slot_row)
    give_back(chunks - 1)

    def arrived(k, carry):
        b = lax.rem(me + k, blocks)
        remote(
            result.at[b], att.at[b], back_send_sem.at[b], back_recv_sem.at[b],
            group_device(b, reps),
        ).wait_recv()
        return carry

    lax.fori_loop(1, blocks, arrived, 0)
    attended = att[...].reshape(D, T).astype(F32).T.astype(BF16)
    mixed = (
        residual_ref[...].astype(F32)
        + jnp.dot(attended, proj_ref[...], preferred_element_type=F32)
    ).astype(BF16)
    mixed_f = mixed.astype(F32)
    inv_rms = lax.rsqrt(jnp.mean(mixed_f * mixed_f, axis=1, keepdims=True) + norm_eps)
    normed = (mixed_f * inv_rms).astype(BF16)
    last = (((1,), (1,)), ((), ()))
    first = (((0,), (0,)), ((), ()))
    logits = lax.dot_general(normed, router_ref[...], last, preferred_element_type=F32)
    gate = jax.nn.sigmoid(jnp.sum(jnp.where(hits, logits, 0.0), axis=1, keepdims=True))
    scaled = (gate * grad_ref[...].astype(F32)).astype(BF16)

    own_slot = hot_slot(my_c, my_y, my_z)
    hot_all[own_slot] = jnp.concatenate(
        [
            jnp.dot(place_hot, normed, preferred_element_type=F32),
            jnp.dot(place_hot, scaled, preferred_element_type=F32),
        ],
        axis=1,
    ).astype(BF16)
    placed = jnp.dot(place_rows, normed, preferred_element_type=F32) + jnp.dot(
        place_grads, scaled, preferred_element_type=F32
    )
    cold_send[...] = placed.astype(BF16).reshape(experts, PAIR, D)

    def z_copy(k):
        to = lax.rem(my_z + k, DEPTH)
        return remote(
            hot_all.at[own_slot], hot_all.at[own_slot], hz_ssem.at[k - 1], hz_rsem.at[my_z],
            place_of(my_y, to, my_c),
        )

    def z_arrival(z):
        slot = hot_slot(my_c, my_y, z)
        return remote(
            hot_all.at[slot], hot_all.at[slot], hz_ssem.at[0], hz_rsem.at[z],
            place_of(my_y, z, my_c),
        )

    def ring_copy(way, s, z):
        sign = 1 if way == 0 else -1
        block = lax.rem(my_y - sign * s + ys, ys)
        slot = hot_slot(my_c, block, z)
        return remote(
            hot_all.at[slot], hot_all.at[slot], ring_ssem.at[way, s, z], ring_rsem.at[way, s, z],
            place_of(lax.rem(my_y + sign + ys, ys), my_z, my_c),
        )

    def ring_block(way, s):
        sign = 1 if way == 0 else -1
        return lax.rem(my_y - sign * (s + 1) + ys, ys)

    def ring_arrival(way, s, z):
        sign = 1 if way == 0 else -1
        slot = hot_slot(my_c, ring_block(way, s), z)
        return remote(
            hot_all.at[slot], hot_all.at[slot], ring_ssem.at[way, s, z], ring_rsem.at[way, s, z],
            place_of(lax.rem(my_y - sign + ys, ys), my_z, my_c),
        )

    def to_sibling(y, z):
        slot = hot_slot(my_c, y, z)
        return remote(
            hot_all.at[slot], hot_all.at[slot], hc_ssem.at[y, z], hc_rsem.at[y, z],
            place_of(my_y, my_z, 1 - my_c),
        )

    def from_sibling(y, z):
        slot = hot_slot(1 - my_c, y, z)
        return remote(
            hot_all.at[slot], hot_all.at[slot], hc_ssem.at[y, z], hc_rsem.at[y, z],
            place_of(my_y, my_z, 1 - my_c),
        )

    def ring_start(t):
        z = lax.rem(my_z + t, DEPTH)
        if t:
            z_arrival(z).wait_recv()
        for way in range(2):
            ring_copy(way, 0, z).start()
        to_sibling(my_y, z).start()

    for k in range(1, DEPTH):
        z_copy(k).start()
    ring_start(0)

    def cold_copy(k):
        to = lax.rem(mine + k, experts)
        return remote(
            cold_send.at[to], cold_got.at[mine], cold_ssem.at[to], cold_rsem.at[mine],
            {"expert": to},
        )

    def start_cold(k, carry):
        cold_copy(k).start()
        return carry

    lax.fori_loop(1, experts, start_cold, 0)
    cold_got[mine] = cold_send[mine]
    ways = (ys // 2, ys - 1 - ys // 2)
    for t in range(1, DEPTH):
        ring_start(t)

    def ring_step(s):
        for t in range(DEPTH):
            z = lax.rem(my_z + t, DEPTH)
            for way in range(2):
                if s < ways[way]:
                    ring_arrival(way, s, z).wait_recv()
                    if s + 1 < ways[way]:
                        ring_copy(way, s + 1, z).start()
                    to_sibling(ring_block(way, s), z).start()

    def cold_here(k, carry):
        b = lax.rem(mine + k, experts)
        remote(
            cold_send.at[b], cold_got.at[b], cold_ssem.at[b], cold_rsem.at[b], {"expert": b}
        ).wait_recv()
        return carry

    load_up.wait()
    load_down.wait()
    up = up_ref[...]
    down = down_ref[...]

    def expert_pass(tokens, grads_in):
        pre = jnp.dot(tokens, up, preferred_element_type=F32)
        sig = jax.nn.sigmoid(pre)
        activated = (pre * sig).astype(BF16)
        made = jnp.dot(activated, down, preferred_element_type=F32).astype(BF16)
        act_grad = lax.dot_general(grads_in, down, last, preferred_element_type=F32)
        pre_grad = (act_grad * sig * (1.0 + pre * (1.0 - sig))).astype(BF16)
        token_grad = lax.dot_general(pre_grad, up, last, preferred_element_type=F32).astype(BF16)
        return activated, pre_grad, made, token_grad

    owner = (hot_id == mine).astype(F32)

    def core_copy(b):
        return remote(
            hot_res.at[pl.ds(hot_slot(1 - my_c, b, 0), DEPTH)],
            core_got.at[pl.ds(b * DEPTH, DEPTH)], core_ssem.at[b], core_rsem.at[b],
            place_of(my_y, my_z, 1 - my_c),
        )

    def pair_of(p):
        if p + 1 < ways[0]:
            return [lax.rem(my_y - p - 1 + ys, ys), lax.rem(my_y + p + 1, ys)]
        return [lax.rem(my_y + ways[0], ys), my_y]

    def hot_pass(p):
        where = []
        for b in pair_of(p):
            for z in range(DEPTH):
                from_sibling(b, z).wait_recv()
            where += [hot_slot(c, b, 0) for c in range(CORES)]
        size = DEPTH * HOT
        both = jnp.concatenate(
            [hot_all[pl.ds(slot, DEPTH)].reshape(size, 2 * D) for slot in where], axis=0
        )
        activated, pre_grad, hot_made, hot_grad = expert_pass(both[:, 0:D], both[:, D : 2 * D])
        kept_act = (activated.astype(F32) * owner).astype(BF16)
        kept_pre = (pre_grad.astype(F32) * owner).astype(BF16)
        for i, slot in enumerate(where):
            rows = slice(i * size, (i + 1) * size)
            here = pl.ds(slot, DEPTH)
            hot_res[here, :, 0:D] = hot_made[rows].reshape(DEPTH, HOT, D)
            hot_res[here, :, D : 2 * D] = hot_grad[rows].reshape(DEPTH, HOT, D)
            act_ref[here] = kept_act[rows].reshape(DEPTH, HOT, FF)
            pre_ref[here] = kept_pre[rows].reshape(DEPTH, HOT, FF)

    def core_start(p):
        for b in pair_of(p):
            core_copy(b).start()

    hot_y = hot_id // row_size
    hot_z = lax.rem(hot_id, row_size) // CORES
    hot_c = lax.rem(hot_id, CORES)

    def y_copy(b):
        return remote(
            y_send.at[b], y_got.at[my_y], y_ssem.at[b], y_rsem.at[my_y],
            place_of(b, my_z, my_c),
        )

    def y_fill(p):
        for b in pair_of(p):
            remote(
                hot_res.at[pl.ds(hot_slot(1 - my_c, b, 0), DEPTH)],
                core_got.at[pl.ds(b * DEPTH, DEPTH)], core_ssem.at[b], core_rsem.at[b],
                place_of(my_y, my_z, 1 - my_c),
            ).wait_recv()
            own = hot_res[pl.ds(hot_slot(my_c, b, 0), DEPTH)].astype(F32)
            other = core_got[pl.ds(b * DEPTH, DEPTH)].astype(F32)
            y_send[b] = jnp.where(hot_c == my_c, own, other).astype(BF16)

    def y_start(p):
        here = pair_of(p)
        if p + 1 == ways[0]:
            here = here[:1]
        for b in here:
            y_copy(b).start()

    ring_step(0)
    ring_step(1)
    hot_pass(0)
    core_start(0)
    ring_step(2)
    lax.fori_loop(1, experts, cold_here, 0)
    cold_count = experts * CAP
    packed = cold_got[...].reshape(slots, D)
    cold_i = lax.broadcasted_iota(jnp.int32, (cold_count, slots), 0)
    pair_i = lax.broadcasted_iota(jnp.int32, (cold_count, slots), 1)
    spot = (cold_i // CAP) * PAIR + lax.rem(cold_i, CAP)
    take_rows = ones(pair_i == spot)
    take_grads = ones(pair_i == spot + CAP)
    cold_rows = jnp.dot(take_rows, packed, preferred_element_type=F32).astype(BF16)
    cold_grads = jnp.dot(take_grads, packed, preferred_element_type=F32).astype(BF16)
    cold_act, cold_pre, made, token_grad = expert_pass(cold_rows, cold_grads)
    repacked = lax.dot_general(take_rows, made, first, preferred_element_type=F32)
    repacked = repacked + lax.dot_general(
        take_grads, token_grad, first, preferred_element_type=F32
    )
    made_send[...] = repacked.astype(BF16).reshape(experts, PAIR, D)
    grad_up = lax.dot_general(cold_rows, cold_pre, first, preferred_element_type=F32)
    grad_down = lax.dot_general(cold_act, cold_grads, first, preferred_element_type=F32)

    def made_copy(k):
        to = lax.rem(mine + k, experts)
        return remote(
            made_send.at[to], made_got.at[mine], made_ssem.at[to], made_rsem.at[mine],
            {"expert": to},
        )

    def start_made(k, carry):
        made_copy(k).start()
        return carry

    lax.fori_loop(1, experts, start_made, 0)
    made_got[mine] = made_send[mine]
    for p in range(1, ways[0] - 1):
        if p > 1:
            ring_step(p + 1)
        hot_pass(p)
        y_fill(p - 1)
        core_start(p)
        y_start(p - 1)
    hot_pass(ways[0] - 1)
    y_fill(ways[0] - 2)
    core_start(ways[0] - 1)
    y_start(ways[0] - 2)
    share = D // blocks

    def store_grad(m, grad):
        for j in range(blocks):
            grads[m, j % reps, j // reps] = grad[j * share : (j + 1) * share].astype(BF16)

    hot_count = experts * HOT
    hot_rows = hot_all[...].reshape(hot_count, 2 * D)
    grad_up = grad_up + lax.dot_general(
        hot_rows[:, 0:D], pre_ref[...].reshape(hot_count, FF), first, preferred_element_type=F32
    )
    store_grad(0, grad_up)

    def along_x(m, k):
        to = lax.rem(my_rep + k, reps)
        return remote(
            grads.at[m, to], got_x.at[m, k - 1], x_ssem.at[m, k - 1], x_rsem.at[m, k - 1],
            {"rep": to},
        )

    def along_z(m, k):
        to = lax.rem(my_seq + k, seqs)
        return remote(
            part.at[m, to], got_zz.at[m, k - 1], zz_ssem.at[m, k - 1], zz_rsem.at[m, k - 1],
            {"seq": to},
        )

    for k in range(1, reps):
        along_x(0, k).start()
    y_fill(ways[0] - 1)
    grad_down = grad_down + lax.dot_general(
        act_ref[...].reshape(hot_count, FF), hot_rows[:, D : 2 * D], first,
        preferred_element_type=F32,
    )
    y_start(ways[0] - 1)
    store_grad(1, grad_down)
    y_got[my_y] = y_send[my_y]
    for k in range(1, reps):
        along_x(1, k).start()
    for m in range(2):
        for k in range(1, reps):
            along_x(m, k).wait_recv()
        for p in range(seqs):
            total = grads[m, my_rep, p].astype(F32)
            for k in range(1, reps):
                total = total + got_x[m, k - 1, p].astype(F32)
            part[m, p] = total.astype(BF16)
        for k in range(1, seqs):
            along_z(m, k).start()
    for k in range(1, ys):
        b = lax.rem(my_y + k, ys)
        remote(
            y_send.at[b], y_got.at[b], y_ssem.at[b], y_rsem.at[b], place_of(b, my_z, my_c)
        ).wait_recv()
    for z in range(DEPTH):
        kept = y_got[0, z].astype(F32)
        for y in range(1, ys):
            kept = jnp.where(hot_y == y, y_got[y, z].astype(F32), kept)
        z_send[z] = kept.astype(BF16)

    def made_here(k, carry):
        b = lax.rem(mine + k, experts)
        remote(
            made_send.at[b], made_got.at[b], made_ssem.at[b], made_rsem.at[b], {"expert": b}
        ).wait_recv()
        return carry

    lax.fori_loop(1, experts, made_here, 0)

    def down_copy(k):
        to = lax.rem(my_z + k, DEPTH)
        return remote(
            z_send.at[to], z_got.at[my_z], z_ssem.at[to], z_rsem.at[my_z],
            place_of(my_y, to, my_c),
        )

    for k in range(1, DEPTH):
        down_copy(k).start()
    z_got[my_z] = z_send[my_z]
    slot_lane = lax.broadcasted_iota(jnp.int32, (T, slots), 1)
    back = made_got[...].reshape(slots, D)
    result_f = jnp.dot(ones(slot_lane == cold_slot_col), back, preferred_element_type=F32)
    normed_grad = jnp.dot(
        ones(slot_lane == cold_slot_col + CAP), back, preferred_element_type=F32
    )
    router_cols = jnp.dot(ones(hits), router_ref[...], preferred_element_type=F32)
    for k in range(1, DEPTH):
        b = lax.rem(my_z + k, DEPTH)
        remote(
            z_send.at[b], z_got.at[b], z_ssem.at[b], z_rsem.at[b], place_of(my_y, b, my_c)
        ).wait_recv()
    kept = z_got[0].astype(F32)
    for z in range(1, DEPTH):
        kept = jnp.where(hot_z == z, z_got[z].astype(F32), kept)
    kept = kept.astype(BF16)
    pick_hot = ones(lax.broadcasted_iota(jnp.int32, (T, HOT), 1) == hot_slot_col)
    result_f = result_f + jnp.dot(pick_hot, kept[:, 0:D], preferred_element_type=F32)
    normed_grad = normed_grad + jnp.dot(
        pick_hot, kept[:, D : 2 * D], preferred_element_type=F32
    )
    grad_f = grad_ref[...].astype(F32)
    out_ref[...] = (mixed_f + gate * result_f).astype(BF16)
    gate_grad = jnp.sum(grad_f * result_f, axis=1, keepdims=True)
    logit_grad = gate_grad * gate * (1.0 - gate)
    total_grad = normed_grad + logit_grad * router_cols
    mean_term = jnp.mean(total_grad * mixed_f, axis=1, keepdims=True)
    input_grad = inv_rms * total_grad - mixed_f * inv_rms * inv_rms * inv_rms * mean_term
    grad_mixed_ref[...] = (grad_f + input_grad).astype(BF16)
    for m, ref in enumerate((share_in_ref, share_out_ref)):
        for k in range(1, seqs):
            along_z(m, k).wait_recv()
        total = part[m, my_seq].astype(F32)
        for k in range(1, seqs):
            total = total + got_zz[m, k - 1].astype(F32)
        ref[...] = total

    def sent_group(k, carry):
        outgoing(k).wait_send()
        returning(lax.rem(me + k, blocks)).wait_send()
        return carry

    def sent_experts(k, carry):
        cold_copy(k).wait_send()
        made_copy(k).wait_send()
        return carry

    lax.fori_loop(1, blocks, sent_group, 0)
    lax.fori_loop(1, experts, sent_experts, 0)
    for k in range(1, DEPTH):
        z_copy(k).wait_send()
        down_copy(k).wait_send()
    for way in range(2):
        for s in range(ways[way]):
            for z in range(DEPTH):
                ring_copy(way, s, z).wait_send()
    for y in range(ys):
        for z in range(DEPTH):
            to_sibling(y, z).wait_send()
    for b in range(ys):
        core_copy(b).wait_send()
    for k in range(1, ys):
        y_copy(lax.rem(my_y + k, ys)).wait_send()
    for m in range(2):
        for k in range(1, reps):
            along_x(m, k).wait_send()
        for k in range(1, seqs):
            along_z(m, k).wait_send()


def local(
    query_rows, key_rows, value_rows, doc_lengths, residual, out_proj, router, expert_choice,
    weight_in, weight_out, grad_out,
):
    seqs, reps = lax.axis_size("seq"), lax.axis_size("rep")
    blocks = seqs * reps
    experts = router.shape[1]
    share = D // blocks
    ys = experts // (CORES * DEPTH)
    dma = pltpu.SemaphoreType.DMA
    buffers = [
        (blocks, 3 * HD, T), (blocks, 3 * HD, T), (blocks, HD, T), (blocks, HD, T),
        (HD, blocks * T), (blocks * T, HD), (HD, blocks * T), (D, FF), (FF, D),
        (experts, PAIR, D), (experts, PAIR, D), (experts, PAIR, D), (experts, PAIR, D),
        (experts, HOT, 2 * D), (experts, HOT, 2 * D), (experts // CORES, HOT, 2 * D),
        (ys, DEPTH, HOT, 2 * D), (ys, DEPTH, HOT, 2 * D), (DEPTH, HOT, 2 * D),
        (DEPTH, HOT, 2 * D), (experts, HOT, FF), (experts, HOT, FF),
        (2, reps, seqs, share, FF), (2, reps - 1, seqs, share, FF), (2, seqs, share, FF),
        (2, seqs - 1, share, FF),
    ]
    semaphores = (
        [dma((2,))] + [dma((blocks,))] * 4 + [dma((experts,))] * 4
        + [dma((DEPTH - 1,)), dma((DEPTH,))]
        + [dma((2, ys // 2, DEPTH))] * 2 + [dma((ys, DEPTH))] * 2
        + [dma((ys,))] * 4 + [dma((DEPTH,))] * 2
        + [dma((2, reps - 1))] * 2 + [dma((2, seqs - 1))] * 2
    )
    anywhere = pl.BlockSpec(memory_space=pl.ANY)
    outs = pl.pallas_call(
        functools.partial(step_body, seqs, reps, experts),
        out_shape=(jax.ShapeDtypeStruct((T, D), BF16),) * 2
        + (jax.ShapeDtypeStruct((share, FF), F32),) * 2,
        in_specs=[pl.BlockSpec(memory_space=pltpu.SMEM)] + [VMEM] * 8 + [anywhere] * 2,
        out_specs=(VMEM,) * 4,
        scratch_shapes=[pltpu.VMEM(shape, BF16) for shape in buffers] + semaphores,
        compiler_params=pltpu.CompilerParams(collective_id=1, has_side_effects=True),
        name="step",
    )(
        doc_lengths, query_rows[0], key_rows[0], value_rows[0], residual[0], out_proj, router.T,
        expert_choice.reshape(1, T), grad_out[0], weight_in[0], weight_out[0],
    )
    return tuple(out[None] for out in outs)


def solution(mesh):
    rows = P("expert", ("seq", "rep"), None)
    weights = P("expert", None, None)
    in_specs = (
        rows, rows, rows, P("expert", None), rows, P(), P(), rows, weights, weights, rows,
    )
    return jax.shard_map(
        local, mesh=mesh, in_specs=in_specs, out_specs=(rows,) * 4, check_vma=False
    )
```
